32 devices in a mesh: dp: 4 (over y, core), cells: 8 (over z, x).
Axes of the slice: x: 2, y: 2, z: 4, core: 2. Of those that a mesh axis runs over, the one named last changes fastest.
Arguments:
- sensitivity: float32 [8192, 12288], P('dp', 'cells'), may hold values from -0.0546875 to 0.0546875
- observed: float32 [8192, 256], P('dp'), may hold values from -6 to 6
- models: float32 [12288, 256], P('cells'), may hold values from -6 to 6
- neighbour_map: int32 [4, 768], replicated, may hold values from 0 to 767, as said below
- edge_mask: int32 [12288], P('cells'), may hold values 0 or 1
Outputs:
- updated: float32 [12288, 256], P('cells')
The draws below stay inside these ranges and needn't reach their ends.
Inputs may be any that keep to these rules, and one draw needn't show every extreme that they name: `neighbour_map`: each row k maps every cell of a periodic 32 by 24 plane grid, numbered in a drawn order, to its neighbour in one of the four grid directions; every row is a permutation.
All inputs are finite; a program needn't handle non-finite values. No bound on the sum of `edge_mask` on one device may be relied on, other than what follows from the above.
Results may differ from the reference program's by a relative error of at most 0.0001.
Values sent between devices are 32-bit elements; how exact they have to be, the bound alone decides.
A program may use at most 128 MiB of HBM per device.

```python
import jax
import jax.numpy as jnp
from jax import lax

NDATA = 8192
PX = 32
PY = 24
SOLS = 256
ITERS = 2
PLANE = 768
NCELL = 12288


def draw_neighbour_map(key, part):
    total = PX * PY
    labels = jax.random.permutation(jax.random.fold_in(key, 11), total).astype(jnp.int32)
    index = jnp.arange(total, dtype=jnp.int32)
    first = index // PY
    second = index % PY
    targets = [(first + 1) % PX * PY + second, (first + PX - 1) % PX * PY + second, first * PY + (second + 1) % PY, first * PY + (second + PY - 1) % PY]
    rows = []
    for target in targets:
        row = jnp.zeros((total,), jnp.int32).at[labels].set(labels[target])
        rows.append(row)
    return jnp.stack(rows, axis=0)


def set_ends(entries, stream_key, low, largest):
    longest = entries.shape.index(max(entries.shape))
    spots = []
    for shift in (0, 1):
        where = [jax.random.randint(jax.random.fold_in(stream_key, axis), (), 0, length) for axis, length in enumerate(entries.shape)]
        where[longest] = (where[longest] + shift) % entries.shape[longest]
        spots.append(tuple(where))
    return entries.at[spots[0]].set(low).at[spots[1]].set(largest)


def level_of(own_key, shape, shards, least, high):
    def one(dim, parts):
        steps = jax.random.uniform(jax.random.fold_in(jax.random.fold_in(own_key, 6), dim), (parts,), jnp.float32, least / len(shards), high / len(shards))
        return jnp.repeat(jnp.exp(steps), shape[dim] // parts).reshape((-1,) + (1,) * (len(shape) - dim - 1))

    factor_of = one(*shards[0])
    for cut in shards[1:]:
        factor_of = factor_of * one(*cut)
    return factor_of


def centred(rng, shape, spread, most, shards=(), kind=jnp.bfloat16):
    values = jax.random.normal(rng, shape, jnp.float32) * spread
    if len(shards) > 0:
        values = level_of(rng, shape, shards, -0.22, 0.18) * values
    return jnp.clip(values, min=-most, max=most).astype(kind)


def setup_inputs(seed: int = 0) -> dict:
    key_of = jax.random.split(jax.random.key(seed), 6)
    return {
        "sensitivity": centred(key_of[0], (NDATA, NCELL), NCELL ** -0.5, 0.0546875, ((0, 4), (1, 8)), jnp.float32),
        "observed": centred(key_of[1], (NDATA, SOLS), 1.0, 6.0, ((0, 4),), jnp.float32),
        "models": centred(key_of[2], (NCELL, SOLS), 1.0, 6.0, ((0, 8),), jnp.float32),
        "neighbour_map": draw_neighbour_map(jax.random.fold_in(key_of[5], 71), 0),
        "edge_mask": set_ends((jax.random.randint(key_of[4], (NCELL,), 0, 4) < 1).astype(jnp.int32), jax.random.fold_in(key_of[4], 1), 0, 1),
    }


def smooth_all(current, neighbour_map, edge_mask):
    count = current.shape[0] // PLANE
    planes = current.reshape(count, PLANE, current.shape[1])
    zero_plane = jnp.zeros((1, PLANE, current.shape[1]), jnp.float32)
    above = jnp.concatenate([zero_plane, planes[:-1]], axis=0)
    below = jnp.concatenate([planes[1:], zero_plane], axis=0)
    total = jnp.zeros_like(planes)
    for other in (above, below):
        diff = other - planes
        total = total + diff / jnp.sqrt(1.0 + diff * diff)
    for k in range(4):
        other = jnp.take(planes, neighbour_map[k], axis=1)
        diff = other - planes
        total = total + diff / jnp.sqrt(1.0 + diff * diff)
    scale = 1.0 - 0.75 * edge_mask.astype(jnp.float32).reshape(count, PLANE, 1)
    return (total * scale).reshape(current.shape)

def reference(sensitivity, observed, models, neighbour_map, edge_mask):
    current = models
    for step in range(ITERS):
        predicted = jnp.dot(sensitivity, current, precision=lax.Precision.HIGHEST, preferred_element_type=jnp.float32)
        misfit = predicted - observed
        weighted = misfit / jnp.maximum(jnp.abs(misfit), 1.0)
        gradient = lax.dot_general(sensitivity, weighted, (((0,), (0,)), ((), ())), precision=lax.Precision.HIGHEST, preferred_element_type=jnp.float32)
        current = current - 1.0 * gradient + 0.05 * smooth_all(current, neighbour_map, edge_mask)
    return current
```

```python
import functools

import jax
import jax.numpy as jnp
from jax import lax
from jax.experimental import pallas as pl
from jax.experimental.pallas import tpu as pltpu
from jax.sharding import PartitionSpec as P

ITERS = 2
CHUNK = 512
GROUPS = 4
CELL_AT = (0, 4, 7, 10, 13, 17)
BACK_LAG = 1
DP_AT = (0, 2, 5, 7)
PIECES = 4
HALO_LAG = 0
HALO_STRIDE = 2
SMOOTH_LAG = 12
STRIDE = 2
TURNED = 0
ORDER = (1, 0)
LANES = 128
F32 = jnp.float32
BF16 = jnp.bfloat16


def split(x):
    hi = x.astype(BF16)
    return hi, (x - hi.astype(F32)).astype(BF16)


def digits_of(count):
    digits = []
    while count > 1:
        digits.append(2)
        count //= 2
    return digits


def dot(a, b, dims):
    return lax.dot_general(a, b, (dims, ((), ())), preferred_element_type=F32)


def over(x, n):
    if n & (n - 1):
        return lax.div(x, n), lax.rem(x, n)
    return lax.shift_right_logical(x, n.bit_length() - 1), lax.bitwise_and(x, n - 1)


def timetable(times, stages):
    times = list(times)
    while len(times) <= stages:
        times.append(times[-1] + 3)
    return times


def lanes(start, size):
    return pl.ds(pl.multiple_of(start, LANES), size)


class Sum:
    def __init__(self, axis, digits, size, cols, sends, recvs, order=(), sem=0):
        strides = [1]
        for base in digits[:-1]:
            strides.append(strides[-1] * base)
        order = list(order) + list(range(len(order), len(digits)))
        self.axis, self.cols, self.pitch = axis, cols, size
        self.sends, self.recvs, self.sem = sends, recvs, sem
        self.last = len(digits) - 1
        self.stages = 2 * self.last + 1
        me = lax.axis_index(axis)
        self.peer, self.away, self.off, self.size = [], [], [0], [size]
        for b in range(len(digits)):
            stride = strides[order[b]]
            mine = (me // stride) % 2
            self.peer.append(me + (1 - 2 * mine) * stride)
            self.mine = mine
            if b < self.last:
                piece = self.size[b] // 2
                self.away.append(self.off[b] + (1 - mine) * piece)
                self.off.append(self.off[b] + mine * piece)
                self.size.append(piece)

    def kept(self, chunk, b):
        return lanes(chunk * self.pitch + self.off[b + 1], self.size[b + 1])

    def landed(self, chunk, b):
        size = self.size[min(b + 1, self.last)]
        return lanes(chunk * self.pitch + self.pitch - self.size[b], size)

    def remote(self, source, target, slot, sem, peer):
        return pltpu.make_async_remote_copy(
            src_ref=source,
            dst_ref=target,
            send_sem=self.sends.at[self.sem + sem, slot],
            recv_sem=self.recvs.at[self.sem + sem, slot],
            device_id={self.axis: peer},
            device_id_type=pl.DeviceIdType.MESH,
        )

    def move(self, s, chunk, slot, data, land, result):
        last = self.last
        if s < last:
            away = lanes(chunk * self.pitch + self.away[s], self.size[s + 1])
            source, target, b = data.at[self.cols, away], land.at[self.cols, self.landed(chunk, s)], s
        elif s == last:
            source, target, b = data.at[self.cols, self.kept(chunk, last - 1)], land.at[self.cols, self.landed(chunk, last)], last
        else:
            b = 2 * last - s
            source = target = result.at[self.cols, self.kept(chunk, b)]
        return self.remote(source, target, slot, s, self.peer[b])

    def stage(self, s, chunk, slot, data, land, result, finish, adjust=None):
        last = self.last
        if s > 0:
            self.move(s - 1, chunk, slot, data, land, result).wait()
        if 0 < s <= last:
            at = self.kept(chunk, s - 1)
            data[self.cols, at] += land[self.cols, self.landed(chunk, s - 1)]
            if s == last and adjust is not None:
                adjust()
        elif s == last + 1:
            at = self.kept(chunk, last - 1)
            finish(self.cols, at, data[self.cols, at] + land[self.cols, self.landed(chunk, last)])
        if s < self.stages:
            self.move(s, chunk, slot, data, land, result).start()


def body(sizes, plane, sens_hbm, obs_hbm, models_hbm, near_ref, mask_ref, out_hbm,
         sens, s_high, s_low, obs_raw, obs, part, land, weighted, grad, gland, flat, state, wide,
         pick, smooth, rim, load_sem, obs_sem, edge_sem, c_send, c_recv, d_send, d_recv, h_send, h_recv):
    n_dp, n_cells = sizes
    ndata, ncell = sens.shape
    groups, width, _ = grad.shape
    per = LANES // width
    me = lax.axis_index("cells")
    chunks = load_sem.shape[0]
    rows = ndata // chunks
    parts = ncell // plane
    prow = ncell // parts
    cell_digits, dp_digits = digits_of(n_cells), digits_of(n_dp)
    straight = width - TURNED
    cells = Sum("cells", cell_digits, rows, pl.ds(0, straight), c_send, c_recv)
    ways = [cells]
    if TURNED:
        order = ORDER if len(cell_digits) >= len(ORDER) else ()
        ways.insert(0, Sum("cells", cell_digits, rows, pl.ds(straight, TURNED), c_send, c_recv, order, cells.stages))
    dp = Sum("dp", dp_digits, prow, pl.ds(0, width), d_send, d_recv)
    seg = dp.size[-1]
    inner = dp.off[-1]
    side = dp.mine
    own = side * prow + inner
    units = groups * chunks
    span = STRIDE * chunks
    cell_at, dp_at = timetable(CELL_AT, cells.stages), timetable(DP_AT, dp.stages)
    behind = cell_at[cells.stages] + BACK_LAG
    delay = span - STRIDE + behind + 1
    done = delay + parts + dp_at[dp.stages]
    period = max(STRIDE * units, done)
    slots = (ITERS - 1) * period + (groups - 1) * span + done
    nn, nt = ((1,), (0,)), ((1,), (1,))

    def load(c):
        at = pl.ds(pl.multiple_of(c * rows, LANES), rows)
        return pltpu.make_async_copy(sens_hbm.at[at], sens.at[at], load_sem.at[c])

    def enter(p):
        at = lanes(p * LANES, LANES)
        return pltpu.make_async_copy(models_hbm.at[:, at], flat.at[:, at], edge_sem.at[p])

    def leave(p):
        at = lanes(p * LANES, LANES)
        return pltpu.make_async_copy(flat.at[:, at], out_hbm.at[:, at], edge_sem.at[p])

    def watch(p):
        at = lanes(p * LANES, LANES)
        return pltpu.make_async_copy(obs_hbm.at[:, at], obs_raw.at[:, at], obs_sem.at[p])

    pairs = groups // per
    for p in range(pairs):
        enter(p).start()
    load(0).start()
    for p in range(pairs):
        watch(p).start()
    for c in range(1, chunks):
        load(c).start()

    barrier = pltpu.get_barrier_semaphore()

    def greet(where):
        pl.semaphore_signal(barrier, inc=1, device_id=where, device_id_type=pl.DeviceIdType.MESH)

    for peer in cells.peer:
        greet({"cells": peer})
    for peer in dp.peer:
        greet({"dp": peer})

    has_under, has_over = me > 0, me < n_cells - 1

    @pl.when(has_under)
    def _():
        greet({"cells": me - 1})

    @pl.when(has_over)
    def _():
        greet({"cells": me + 1})

    upward = side == 0
    gives = (upward & has_over) | (jnp.logical_not(upward) & has_under)
    takes = (upward & has_under) | (jnp.logical_not(upward) & has_over)

    @pl.when(jnp.logical_not(takes))
    def _():
        rim[...] = jnp.zeros_like(rim)

    for p in range(pairs):
        enter(p).wait()
        turned = flat[:, p * LANES:(p + 1) * LANES].T
        for i in range(per):
            state[0, p * per + i] = turned[i * width:(i + 1) * width]

    pl.semaphore_wait(
        barrier,
        len(cell_digits) + len(dp_digits) + (me + n_cells - 1) // n_cells + (2 * n_cells - 2 - me) // n_cells,
    )

    def halo(step, g, i):
        source = (1 - side) * (ncell - plane) + inner
        cols = pl.ds(pl.multiple_of(i * (width // PIECES), 8), width // PIECES)
        return pltpu.make_async_remote_copy(
            src_ref=state.at[step, g, cols, lanes(source, seg)],
            dst_ref=rim.at[step, g, cols],
            send_sem=h_send.at[step, g * PIECES + i],
            recv_sem=h_recv.at[step, g * PIECES + i],
            device_id={"cells": me + 1 - 2 * side},
            device_id_type=pl.DeviceIdType.MESH,
        )

    def border(step, g, i):
        @pl.when(gives)
        def _():
            halo(step, g, i).start()

    def predict(step, g, c):
        @pl.when(c == 0)
        def _():
            hi, lo = split(state[step, g])
            wide[g, :width, :] = hi
            wide[g, width:, :] = lo

        at = pl.ds(pl.multiple_of(c * rows, LANES), rows)

        @pl.when((step == 0) & (g == 0))
        def _():
            load(c).wait()
            hi, lo = split(sens[at, :])
            s_high[at, :] = hi
            s_low[at, :] = lo

        both = dot(wide[g], s_high[at, :], nt)
        part[g, :, at] = both[:width] + both[width:] + dot(wide[g, :width, :], s_low[at, :], nt)

    def sight(step, g, c):
        @pl.when((step == 0) & (lax.rem(g, per) == 0))
        def _():
            p = lax.div(g, per)

            @pl.when(c == 0)
            def _():
                watch(p).wait()

            at = lanes(c * rows, rows)
            turned = obs_raw[at, lanes(p * LANES, LANES)].T
            for i in range(per):
                obs[g + i, :, at] = turned[i * width:(i + 1) * width]

    def back(step, g, c):
        @pl.when(c == 0)
        def _():
            grad[g] = jnp.zeros_like(grad[g])

        at = pl.ds(pl.multiple_of(c * rows, LANES), rows)
        hi, lo = split(weighted[g, :, at])
        both = dot(jnp.concatenate([hi, lo], axis=0), s_high[at, :], nn)
        grad[g] += both[:width] + both[width:] + dot(hi, s_low[at, :], nn)

    def smooth_part(step, g, k):
        @pl.when((step == 0) & (g == 0))
        def _():
            row = near_ref[pl.ds(k, 1), lanes(inner, seg)]
            chosen = lax.broadcasted_iota(jnp.int32, (plane, seg), 0) == row
            pick[k] = jnp.where(chosen, 1.0, 0.0).astype(BF16)

        cell = state[step, g, :, lanes(own, seg)]

        def pull(other):
            diff = other - cell
            return diff / jnp.sqrt(1.0 + diff * diff)

        @pl.when(k == 0)
        def _():
            @pl.when(gives)
            def _():
                for i in range(PIECES):
                    halo(step, g, i).wait_send()

            @pl.when(takes)
            def _():
                for i in range(PIECES):
                    halo(step, g, i).wait_recv()

            beside = state[step, g, :, lanes((1 - side) * prow + inner, seg)]
            smooth[g] = pull(rim[step, g]) + pull(beside)

        both = dot(wide[g, :, lanes(side * plane, plane)], pick[k], nn)
        scale = jnp.where(k == 3, 0.05, 1.0) * jnp.where(k == 3, 1.0 - 0.75 * mask_ref[:, lanes(own, seg)].astype(F32), 1.0)
        smooth[g] = (smooth[g] + pull(both[:width] + both[width:])) * scale

    def at_slot(x, count, stride, act):
        step = sum((x >= i * period).astype(jnp.int32) for i in range(1, ITERS))
        g, place = over(x - step * period, span)
        index, wait = over(place, stride)

        @pl.when((x >= 0) & (g < groups) & (index < count) & (wait == 0))
        def _():
            act(step, g, index)

    def cell_stage(s, step, g, c):
        def reweight(cols, at, total):
            misfit = total - obs[g, cols, at]
            weighted[g, cols, at] = misfit / jnp.maximum(jnp.abs(misfit), 1.0)

        for way in ways:
            way.stage(s, c, step * units + g * chunks + c, part.at[g], land.at[step, g], weighted.at[g], reweight)

    def dp_stage(s, step, g, q):
        def blend():
            @pl.when(side == q)
            def _():
                grad[g, :, lanes(own, seg)] -= smooth[g]

        def update(cols, at, total):
            state[step + 1, g, :, at] = state[step, g, :, at] - 1.0 * total

        slot = (step * groups + g) * parts + q
        dp.stage(s, q, slot, grad.at[g], gland.at[step, g], state.at[step + 1, g], update, blend)

    def depart(step, g, i):
        @pl.when((step == ITERS - 1) & (lax.rem(g, per) == per - 1))
        def _():
            p = lax.div(g, per)
            rest = [state[ITERS, g - per + 1 + i] for i in range(per)]
            flat[:, lanes(p * LANES, LANES)] = jnp.concatenate(rest, axis=0).T
            leave(p).start()

    def slot(t, carry):
        for s in reversed(range(cells.stages + 1)):
            at_slot(t - cell_at[s], chunks, STRIDE, functools.partial(cell_stage, s))
        for s in reversed(range(dp.stages + 1)):
            at_slot(t - delay - dp_at[s], parts, 1, functools.partial(dp_stage, s))
        at_slot(t + 1, chunks, STRIDE, predict)
        at_slot(t - HALO_LAG, PIECES, HALO_STRIDE, border)
        at_slot(t, chunks, STRIDE, sight)
        at_slot(t - SMOOTH_LAG, 4, 1, smooth_part)
        at_slot(t - behind, chunks, STRIDE, back)
        at_slot(t - done + 1, 1, 1, depart)
        return carry

    lax.fori_loop(-1, slots, slot, 0)
    for p in range(pairs):
        leave(p).wait()


def invert(n_dp, n_cells, sensitivity, observed, models, neighbour_map, edge_mask):
    ndata, ncell = sensitivity.shape
    total = models.shape[1]
    width = total // GROUPS
    plane = neighbour_map.shape[1]
    nb, nd = 2 * len(digits_of(n_cells)) - 1, 2 * len(digits_of(n_dp)) - 1
    chunks = ndata // max(CHUNK, LANES * n_cells // 2)
    parts = ncell // plane
    seg = ncell // n_dp
    ways = 2 if TURNED else 1
    vmem = pl.BlockSpec(memory_space=pltpu.VMEM)
    hbm = pl.BlockSpec(memory_space=pl.ANY)
    dma = pltpu.SemaphoreType.DMA
    return pl.pallas_call(
        functools.partial(body, (n_dp, n_cells), plane),
        out_shape=jax.ShapeDtypeStruct(models.shape, F32),
        in_specs=[hbm] * 3 + [vmem] * 2,
        out_specs=hbm,
        scratch_shapes=[
            pltpu.VMEM((ndata, ncell), F32),
            pltpu.VMEM((ndata, ncell), BF16),
            pltpu.VMEM((ndata, ncell), BF16),
            pltpu.VMEM((ndata, total), F32),
            pltpu.VMEM((GROUPS, width, ndata), F32),
            pltpu.VMEM((GROUPS, width, ndata), F32),
            pltpu.VMEM((ITERS, GROUPS, width, ndata), F32),
            pltpu.VMEM((GROUPS, width, ndata), F32),
            pltpu.VMEM((GROUPS, width, ncell), F32),
            pltpu.VMEM((ITERS, GROUPS, width, ncell), F32),
            pltpu.VMEM((ncell, total), F32),
            pltpu.VMEM((ITERS + 1, GROUPS, width, ncell), F32),
            pltpu.VMEM((GROUPS, 2 * width, ncell), BF16),
            pltpu.VMEM((4, plane, seg), BF16),
            pltpu.VMEM((GROUPS, width, seg), F32),
            pltpu.VMEM((ITERS, GROUPS, width, seg), F32),
            dma((chunks,)),
            dma((GROUPS * width // LANES,)),
            dma((GROUPS * width // LANES,)),
            dma((ways * nb, ITERS * GROUPS * chunks)),
            dma((ways * nb, ITERS * GROUPS * chunks)),
            dma((nd, ITERS * GROUPS * parts)),
            dma((nd, ITERS * GROUPS * parts)),
            dma((ITERS, GROUPS * PIECES)),
            dma((ITERS, GROUPS * PIECES)),
        ],
        compiler_params=pltpu.CompilerParams(
            collective_id=0, has_side_effects=True, vmem_limit_bytes=63 * 1024 * 1024
        ),
        name="invert",
    )(sensitivity, observed, models, neighbour_map, edge_mask[None, :])


def solution(mesh):
    return jax.shard_map(
        functools.partial(invert, mesh.shape["dp"], mesh.shape["cells"]),
        mesh=mesh,
        in_specs=(P("dp", "cells"), P("dp", None), P("cells", None), P(), P("cells")),
        out_specs=P("cells", None),
        check_vma=False,
    )
```

```python
import functools

import jax
import jax.numpy as jnp
from jax import lax
from jax.experimental import pallas as pl
from jax.experimental.pallas import tpu as pltpu
from jax.sharding import PartitionSpec as P

ITERS = 2
CHUNK = 512
GROUPS = 4
CELL_AT = (0, 3, 6, 9, 12, 15)
BACK_LAG = 1
DP_AT = (0, 2, 5, 7)
PIECES = 4
HALO_LAG = 0
HALO_STRIDE = 2
SMOOTH_LAG = 12
STRIDE = 2
TURNED = 32
LANES = 128
F32 = jnp.float32
BF16 = jnp.bfloat16


def split(x):
    hi = x.astype(BF16)
    return hi, (x - hi.astype(F32)).astype(BF16)


def digits_of(count):
    digits = []
    while count > 1:
        digits.append(2)
        count //= 2
    return digits


def dot(a, b, dims):
    return lax.dot_general(a, b, (dims, ((), ())), preferred_element_type=F32)


def over(x, n):
    if n & (n - 1):
        return lax.div(x, n), lax.rem(x, n)
    return lax.shift_right_logical(x, n.bit_length() - 1), lax.bitwise_and(x, n - 1)


def timetable(times, stages):
    times = list(times)
    while len(times) <= stages:
        times.append(times[-1] + 3)
    return times


def lanes(start, size):
    return pl.ds(pl.multiple_of(start, LANES), size)


class Sum:
    def __init__(self, axis, digits, size, cols, sends, recvs):
        strides = [1]
        for base in digits[:-1]:
            strides.append(strides[-1] * base)
        self.axis, self.cols, self.pitch = axis, cols, size
        self.sends, self.recvs = sends, recvs
        self.last = len(digits) - 1
        self.stages = 2 * self.last + 1
        me = lax.axis_index(axis)
        self.peer, self.away, self.off, self.size = [], [], [0], [size]
        for b in range(len(digits)):
            stride = strides[b]
            mine = (me // stride) % 2
            self.peer.append(me + (1 - 2 * mine) * stride)
            self.mine = mine
            if b < self.last:
                piece = self.size[b] // 2
                self.away.append(self.off[b] + (1 - mine) * piece)
                self.off.append(self.off[b] + mine * piece)
                self.size.append(piece)

    def kept(self, chunk, b):
        return lanes(chunk * self.pitch + self.off[b + 1], self.size[b + 1])

    def landed(self, chunk, b):
        size = self.size[min(b + 1, self.last)]
        return lanes(chunk * self.pitch + self.pitch - self.size[b], size)

    def remote(self, source, target, slot, sem, peer):
        return pltpu.make_async_remote_copy(
            src_ref=source,
            dst_ref=target,
            send_sem=self.sends.at[sem, slot],
            recv_sem=self.recvs.at[sem, slot],
            device_id={self.axis: peer},
            device_id_type=pl.DeviceIdType.MESH,
        )

    def move(self, s, chunk, slot, data, land, result):
        last = self.last
        if s < last:
            away = lanes(chunk * self.pitch + self.away[s], self.size[s + 1])
            source, target, b = data.at[self.cols, away], land.at[self.cols, self.landed(chunk, s)], s
        elif s == last:
            source, target, b = data.at[self.cols, self.kept(chunk, last - 1)], land.at[self.cols, self.landed(chunk, last)], last
        else:
            b = 2 * last - s
            source = target = result.at[self.cols, self.kept(chunk, b)]
        return self.remote(source, target, slot, s, self.peer[b])

    def stage(self, s, chunk, slot, data, land, result, finish, adjust=None):
        last = self.last
        if s > 0:
            self.move(s - 1, chunk, slot, data, land, result).wait()
        if 0 < s <= last:
            at = self.kept(chunk, s - 1)
            data[self.cols, at] += land[self.cols, self.landed(chunk, s - 1)]
            if s == last and adjust is not None:
                adjust()
        elif s == last + 1:
            at = self.kept(chunk, last - 1)
            finish(self.cols, at, data[self.cols, at] + land[self.cols, self.landed(chunk, last)])
        if s < self.stages:
            self.move(s, chunk, slot, data, land, result).start()


class Move:
    def __init__(self, **names):
        self.names = names

    def start(self):
        pltpu.make_async_remote_copy(**self.names).start()

    def wait(self):
        pltpu.make_async_remote_copy(**self.names).wait()

    def wait_send(self):
        pltpu.make_async_remote_copy(**self.names).wait_send()

    def wait_recv(self):
        pltpu.make_async_remote_copy(**self.names).wait_recv()


class Ladder:
    def __init__(self, across, size, cols, sends, recvs, sem):
        self.size, self.half, self.cols, self.across = size, size // 2, cols, across
        self.sends, self.recvs, self.sem = sends, recvs, sem
        self.stages = 5
        me = lax.axis_index("cells")
        z, x = me // 2, me % 2
        self.inner = (z == 1) | (z == 2)
        self.side, self.rank = x, z // 2
        self.beside = me + 1 - 2 * x
        self.mate = me + 2 - 4 * (z % 2)
        self.other = me + 2 - 4 * (z // 2)

    def lane(self, chunk, start, size):
        return lanes(chunk * self.size + start, size)

    def spot(self, chunk, start, size):
        return lanes(chunk * 2 * self.size + start, size)

    def copy(self, source, target, slot, sem, peer):
        return Move(
            src_ref=source,
            dst_ref=target,
            send_sem=self.sends.at[self.sem + sem, slot],
            recv_sem=self.recvs.at[self.sem + sem, slot],
            device_id={"cells": peer},
            device_id_type=pl.DeviceIdType.MESH,
        )

    def stage(self, s, chunk, slot, data, land, result, finish):
        (self.stage_across if self.across else self.stage_along)(s, chunk, slot, data, land, result, finish)

    def stage_across(self, s, chunk, slot, data, land, result, finish):
        cols, half = self.cols, self.half
        mine = self.lane(chunk, self.side * half, half)
        away = self.lane(chunk, (1 - self.side) * half, half)
        spots = [self.spot(chunk, i * half, half) for i in range(3)]
        first = self.copy(data.at[cols, away], land.at[cols, spots[0]], slot, 0, self.beside)
        up = self.copy(data.at[cols, mine], land.at[cols, spots[1]], slot, 1, self.mate)
        swap = self.copy(data.at[cols, mine], land.at[cols, spots[2]], slot, 2, self.other)
        down = self.copy(result.at[cols, mine], result.at[cols, mine], slot, 3, self.mate)
        last = self.copy(result.at[cols, mine], result.at[cols, mine], slot, 4, self.beside)
        inner, outer = pl.when(self.inner), pl.when(jnp.logical_not(self.inner))
        if s == 0:
            first.start()
        elif s == 1:
            first.wait()
            data[cols, mine] += land[cols, spots[0]]
            outer(up.start)
        elif s == 2:
            outer(up.wait_send)

            @inner
            def _():
                up.wait_recv()
                data[cols, mine] += land[cols, spots[1]]
                swap.start()
        elif s == 3:
            @inner
            def _():
                swap.wait()
                finish(cols, mine, data[cols, mine] + land[cols, spots[2]])
                down.start()
                last.start()
        elif s == 4:
            inner(down.wait_send)

            @outer
            def _():
                down.wait_recv()
                last.start()
        else:
            last.wait()

    def stage_along(self, s, chunk, slot, data, land, result, finish):
        cols, half, size = self.cols, self.half, self.size
        whole = self.lane(chunk, 0, size)
        mine = self.lane(chunk, self.rank * half, half)
        away = self.lane(chunk, (1 - self.rank) * half, half)
        begin = self.spot(chunk, 0, size)
        spots = [self.spot(chunk, size + i * half, half) for i in range(2)]
        up = self.copy(data.at[cols, whole], land.at[cols, begin], slot, 0, self.mate)
        first = self.copy(data.at[cols, away], land.at[cols, spots[0]], slot, 1, self.other)
        swap = self.copy(data.at[cols, mine], land.at[cols, spots[1]], slot, 2, self.beside)
        last = self.copy(result.at[cols, mine], result.at[cols, mine], slot, 3, self.other)
        near = self.copy(result.at[cols, mine], result.at[cols, mine], slot, 4, self.mate)
        far = self.copy(result.at[cols, away], result.at[cols, away], slot, 5, self.mate)
        inner, outer = pl.when(self.inner), pl.when(jnp.logical_not(self.inner))
        if s == 0:
            outer(up.start)
        elif s == 1:
            outer(up.wait_send)

            @inner
            def _():
                up.wait_recv()
                data[cols, whole] += land[cols, begin]
                first.start()
        elif s == 2:
            @inner
            def _():
                first.wait()
                data[cols, mine] += land[cols, spots[0]]
                swap.start()
        elif s == 3:
            @inner
            def _():
                swap.wait()
                finish(cols, mine, data[cols, mine] + land[cols, spots[1]])
                last.start()
                near.start()
        elif s == 4:
            inner(near.wait_send)
            outer(near.wait_recv)

            @inner
            def _():
                last.wait()
                far.start()
        else:
            inner(far.wait_send)
            outer(far.wait_recv)


def body(sizes, plane, sens_hbm, obs_hbm, models_hbm, near_ref, mask_ref, out_hbm,
         sens, s_high, s_low, obs_raw, obs, part, land, weighted, grad, gland, flat, state, wide,
         pick, smooth, rim, load_sem, obs_sem, edge_sem, c_send, c_recv, d_send, d_recv, h_send, h_recv):
    n_dp, n_cells = sizes
    ndata, ncell = sens.shape
    groups, width, _ = grad.shape
    per = LANES // width
    me = lax.axis_index("cells")
    chunks = load_sem.shape[0]
    rows = ndata // chunks
    parts = ncell // plane
    prow = ncell // parts
    cell_digits, dp_digits = digits_of(n_cells), digits_of(n_dp)
    if len(cell_digits) == 3:
        straight = width - TURNED
        ways = [
            Ladder(False, rows, pl.ds(straight, TURNED), c_send, c_recv, 5),
            Ladder(True, rows, pl.ds(0, straight), c_send, c_recv, 0),
        ]
    else:
        ways = [Sum("cells", cell_digits, rows, pl.ds(0, width), c_send, c_recv)]
    cells = ways[0]
    dp = Sum("dp", dp_digits, prow, pl.ds(0, width), d_send, d_recv)
    seg = dp.size[-1]
    inner = dp.off[-1]
    side = dp.mine
    own = side * prow + inner
    units = groups * chunks
    span = STRIDE * chunks
    cell_at, dp_at = timetable(CELL_AT, cells.stages), timetable(DP_AT, dp.stages)
    behind = cell_at[cells.stages] + BACK_LAG
    delay = span - STRIDE + behind + 1
    done = delay + parts + dp_at[dp.stages]
    period = max(STRIDE * units, done)
    slots = (ITERS - 1) * period + (groups - 1) * span + done
    nn, nt = ((1,), (0,)), ((1,), (1,))

    def load(c):
        at = pl.ds(pl.multiple_of(c * rows, LANES), rows)
        return pltpu.make_async_copy(sens_hbm.at[at], sens.at[at], load_sem.at[c])

    def enter(p):
        at = lanes(p * LANES, LANES)
        return pltpu.make_async_copy(models_hbm.at[:, at], flat.at[:, at], edge_sem.at[p])

    def leave(p):
        at = lanes(p * LANES, LANES)
        return pltpu.make_async_copy(flat.at[:, at], out_hbm.at[:, at], edge_sem.at[p])

    def watch(p):
        at = lanes(p * LANES, LANES)
        return pltpu.make_async_copy(obs_hbm.at[:, at], obs_raw.at[:, at], obs_sem.at[p])

    pairs = groups // per
    for p in range(pairs):
        enter(p).start()
    load(0).start()
    for p in range(pairs):
        watch(p).start()
    for c in range(1, chunks):
        load(c).start()

    barrier = pltpu.get_barrier_semaphore()

    def greet(where):
        pl.semaphore_signal(barrier, inc=1, device_id=where, device_id_type=pl.DeviceIdType.MESH)

    for d in range(1, n_cells):
        greet({"cells": lax.rem(me + d, n_cells)})
    for peer in dp.peer:
        greet({"dp": peer})

    has_under, has_over = me > 0, me < n_cells - 1

    upward = side == 0
    gives = (upward & has_over) | (jnp.logical_not(upward) & has_under)
    takes = (upward & has_under) | (jnp.logical_not(upward) & has_over)

    @pl.when(jnp.logical_not(takes))
    def _():
        rim[...] = jnp.zeros_like(rim)

    for p in range(pairs):
        enter(p).wait()
        turned = flat[:, p * LANES:(p + 1) * LANES].T
        for i in range(per):
            state[0, p * per + i] = turned[i * width:(i + 1) * width]

    pl.semaphore_wait(barrier, n_cells - 1 + len(dp_digits))

    def halo(step, g, i):
        source = (1 - side) * (ncell - plane) + inner
        cols = pl.ds(pl.multiple_of(i * (width // PIECES), 8), width // PIECES)
        return pltpu.make_async_remote_copy(
            src_ref=state.at[step, g, cols, lanes(source, seg)],
            dst_ref=rim.at[step, g, cols],
            send_sem=h_send.at[step, g * PIECES + i],
            recv_sem=h_recv.at[step, g * PIECES + i],
            device_id={"cells": me + 1 - 2 * side},
            device_id_type=pl.DeviceIdType.MESH,
        )

    def border(step, g, i):
        @pl.when(gives)
        def _():
            halo(step, g, i).start()

    def predict(step, g, c):
        @pl.when(c == 0)
        def _():
            hi, lo = split(state[step, g])
            wide[g, :width, :] = hi
            wide[g, width:, :] = lo

        at = pl.ds(pl.multiple_of(c * rows, LANES), rows)

        @pl.when((step == 0) & (g == 0))
        def _():
            load(c).wait()
            hi, lo = split(sens[at, :])
            s_high[at, :] = hi
            s_low[at, :] = lo

        both = dot(wide[g], s_high[at, :], nt)
        part[g, :, at] = both[:width] + both[width:] + dot(wide[g, :width, :], s_low[at, :], nt)

    def sight(step, g, c):
        @pl.when((step == 0) & (lax.rem(g, per) == 0))
        def _():
            p = lax.div(g, per)

            @pl.when(c == 0)
            def _():
                watch(p).wait()

            at = lanes(c * rows, rows)
            turned = obs_raw[at, lanes(p * LANES, LANES)].T
            for i in range(per):
                obs[g + i, :, at] = turned[i * width:(i + 1) * width]

    def back(step, g, c):
        @pl.when(c == 0)
        def _():
            grad[g] = jnp.zeros_like(grad[g])

        at = pl.ds(pl.multiple_of(c * rows, LANES), rows)
        hi, lo = split(weighted[g, :, at])
        both = dot(jnp.concatenate([hi, lo], axis=0), s_high[at, :], nn)
        grad[g] += both[:width] + both[width:] + dot(hi, s_low[at, :], nn)

    def smooth_part(step, g, k):
        @pl.when((step == 0) & (g == 0))
        def _():
            row = near_ref[pl.ds(k, 1), lanes(inner, seg)]
            chosen = lax.broadcasted_iota(jnp.int32, (plane, seg), 0) == row
            pick[k] = jnp.where(chosen, 1.0, 0.0).astype(BF16)

        cell = state[step, g, :, lanes(own, seg)]

        def pull(other):
            diff = other - cell
            return diff / jnp.sqrt(1.0 + diff * diff)

        @pl.when(k == 0)
        def _():
            @pl.when(gives)
            def _():
                for i in range(PIECES):
                    halo(step, g, i).wait_send()

            @pl.when(takes)
            def _():
                for i in range(PIECES):
                    halo(step, g, i).wait_recv()

            beside = state[step, g, :, lanes((1 - side) * prow + inner, seg)]
            smooth[g] = pull(rim[step, g]) + pull(beside)

        both = dot(wide[g, :, lanes(side * plane, plane)], pick[k], nn)
        scale = jnp.where(k == 3, 0.05, 1.0) * jnp.where(k == 3, 1.0 - 0.75 * mask_ref[:, lanes(own, seg)].astype(F32), 1.0)
        smooth[g] = (smooth[g] + pull(both[:width] + both[width:])) * scale

    def at_slot(x, count, stride, act):
        step = sum((x >= i * period).astype(jnp.int32) for i in range(1, ITERS))
        g, place = over(x - step * period, span)
        index, wait = over(place, stride)

        @pl.when((x >= 0) & (g < groups) & (index < count) & (wait == 0))
        def _():
            act(step, g, index)

    def cell_stage(s, step, g, c):
        def reweight(cols, at, total):
            misfit = total - obs[g, cols, at]
            weighted[g, cols, at] = misfit / jnp.maximum(jnp.abs(misfit), 1.0)

        for way in ways:
            way.stage(s, c, step * units + g * chunks + c, part.at[g], land.at[step, g], weighted.at[g], reweight)

    def dp_stage(s, step, g, q):
        def blend():
            @pl.when(side == q)
            def _():
                grad[g, :, lanes(own, seg)] -= smooth[g]

        def update(cols, at, total):
            state[step + 1, g, :, at] = state[step, g, :, at] - 1.0 * total

        slot = (step * groups + g) * parts + q
        dp.stage(s, q, slot, grad.at[g], gland.at[step, g], state.at[step + 1, g], update, blend)

    def depart(step, g, i):
        @pl.when((step == ITERS - 1) & (lax.rem(g, per) == per - 1))
        def _():
            p = lax.div(g, per)
            rest = [state[ITERS, g - per + 1 + i] for i in range(per)]
            flat[:, lanes(p * LANES, LANES)] = jnp.concatenate(rest, axis=0).T
            leave(p).start()

    def slot(t, carry):
        for s in reversed(range(cells.stages + 1)):
            at_slot(t - cell_at[s], chunks, STRIDE, functools.partial(cell_stage, s))
        for s in reversed(range(dp.stages + 1)):
            at_slot(t - delay - dp_at[s], parts, 1, functools.partial(dp_stage, s))
        at_slot(t + 1, chunks, STRIDE, predict)
        at_slot(t - HALO_LAG, PIECES, HALO_STRIDE, border)
        at_slot(t, chunks, STRIDE, sight)
        at_slot(t - SMOOTH_LAG, 4, 1, smooth_part)
        at_slot(t - behind, chunks, STRIDE, back)
        at_slot(t - done + 1, 1, 1, depart)
        return carry

    lax.fori_loop(-1, slots, slot, 0)
    for p in range(pairs):
        leave(p).wait()


def invert(n_dp, n_cells, sensitivity, observed, models, neighbour_map, edge_mask):
    ndata, ncell = sensitivity.shape
    total = models.shape[1]
    width = total // GROUPS
    plane = neighbour_map.shape[1]
    nb, nd = 2 * len(digits_of(n_cells)) - 1, 2 * len(digits_of(n_dp)) - 1
    chunks = ndata // max(CHUNK, LANES * n_cells // 2)
    parts = ncell // plane
    seg = ncell // n_dp
    copies = 11 if n_cells == 8 else nb
    vmem = pl.BlockSpec(memory_space=pltpu.VMEM)
    hbm = pl.BlockSpec(memory_space=pl.ANY)
    dma = pltpu.SemaphoreType.DMA
    return pl.pallas_call(
        functools.partial(body, (n_dp, n_cells), plane),
        out_shape=jax.ShapeDtypeStruct(models.shape, F32),
        in_specs=[hbm] * 3 + [vmem] * 2,
        out_specs=hbm,
        scratch_shapes=[
            pltpu.VMEM((ndata, ncell), F32),
            pltpu.VMEM((ndata, ncell), BF16),
            pltpu.VMEM((ndata, ncell), BF16),
            pltpu.VMEM((ndata, total), F32),
            pltpu.VMEM((GROUPS, width, ndata), F32),
            pltpu.VMEM((GROUPS, width, ndata), F32),
            pltpu.VMEM((ITERS, GROUPS, width, 2 * ndata), F32),
            pltpu.VMEM((GROUPS, width, ndata), F32),
            pltpu.VMEM((GROUPS, width, ncell), F32),
            pltpu.VMEM((ITERS, GROUPS, width, ncell), F32),
            pltpu.VMEM((ncell, total), F32),
            pltpu.VMEM((ITERS + 1, GROUPS, width, ncell), F32),
            pltpu.VMEM((GROUPS, 2 * width, ncell), BF16),
            pltpu.VMEM((4, plane, seg), BF16),
            pltpu.VMEM((GROUPS, width, seg), F32),
            pltpu.VMEM((ITERS, GROUPS, width, seg), F32),
            dma((chunks,)),
            dma((GROUPS * width // LANES,)),
            dma((GROUPS * width // LANES,)),
            dma((copies, ITERS * GROUPS * chunks)),
            dma((copies, ITERS * GROUPS * chunks)),
            dma((nd, ITERS * GROUPS * parts)),
            dma((nd, ITERS * GROUPS * parts)),
            dma((ITERS, GROUPS * PIECES)),
            dma((ITERS, GROUPS * PIECES)),
        ],
        compiler_params=pltpu.CompilerParams(
            collective_id=0, has_side_effects=True, vmem_limit_bytes=63 * 1024 * 1024
        ),
        name="invert",
    )(sensitivity, observed, models, neighbour_map, edge_mask[None, :])


def solution(mesh):
    return jax.shard_map(
        functools.partial(invert, mesh.shape["dp"], mesh.shape["cells"]),
        mesh=mesh,
        in_specs=(P("dp", "cells"), P("dp", None), P("cells", None), P(), P("cells")),
        out_specs=P("cells", None),
        check_vma=False,
    )
```

```python
import functools

import jax
import jax.numpy as jnp
from jax import lax
from jax.experimental import pallas as pl
from jax.experimental.pallas import tpu as pltpu
from jax.sharding import PartitionSpec as P

ITERS = 2
CHUNK = 512
LOAD = 256
TURN_LAG = 0
GROUPS = 4
CELL_AT = (0, 3, 6, 9, 12, 15)
BACK_LAG = 1
DP_AT = (0, 2, 5, 7)
PIECES = 4
HALO_LAG = 0
HALO_STRIDE = 2
SMOOTH_LAG = 11
STRIDE = 2
TURNED = 32
LANES = 128
F32 = jnp.float32
BF16 = jnp.bfloat16


def split(x):
    hi = x.astype(BF16)
    return hi, (x - hi.astype(F32)).astype(BF16)


def digits_of(count):
    digits = []
    while count > 1:
        digits.append(2)
        count //= 2
    return digits


def dot(a, b, dims):
    return lax.dot_general(a, b, (dims, ((), ())), preferred_element_type=F32)


def over(x, n):
    if n & (n - 1):
        return lax.div(x, n), lax.rem(x, n)
    return lax.shift_right_logical(x, n.bit_length() - 1), lax.bitwise_and(x, n - 1)


def timetable(times, stages):
    times = list(times)
    while len(times) <= stages:
        times.append(times[-1] + 3)
    return times


def lanes(start, size):
    return pl.ds(pl.multiple_of(start, LANES), size)


class Sum:
    def __init__(self, axis, digits, size, cols, sends, recvs):
        strides = [1]
        for base in digits[:-1]:
            strides.append(strides[-1] * base)
        self.axis, self.cols, self.pitch = axis, cols, size
        self.sends, self.recvs = sends, recvs
        self.last = len(digits) - 1
        self.stages = 2 * self.last + 1
        me = lax.axis_index(axis)
        self.peer, self.away, self.off, self.size = [], [], [0], [size]
        for b in range(len(digits)):
            stride = strides[b]
            mine = (me // stride) % 2
            self.peer.append(me + (1 - 2 * mine) * stride)
            self.mine = mine
            if b < self.last:
                piece = self.size[b] // 2
                self.away.append(self.off[b] + (1 - mine) * piece)
                self.off.append(self.off[b] + mine * piece)
                self.size.append(piece)

    def kept(self, chunk, b):
        return lanes(chunk * self.pitch + self.off[b + 1], self.size[b + 1])

    def landed(self, chunk, b):
        size = self.size[min(b + 1, self.last)]
        return lanes(chunk * self.pitch + self.pitch - self.size[b], size)

    def remote(self, source, target, slot, sem, peer):
        return pltpu.make_async_remote_copy(
            src_ref=source,
            dst_ref=target,
            send_sem=self.sends.at[sem, slot],
            recv_sem=self.recvs.at[sem, slot],
            device_id={self.axis: peer},
            device_id_type=pl.DeviceIdType.MESH,
        )

    def move(self, s, chunk, slot, data, land, result):
        last = self.last
        if s < last:
            away = lanes(chunk * self.pitch + self.away[s], self.size[s + 1])
            source, target, b = data.at[self.cols, away], land.at[self.cols, self.landed(chunk, s)], s
        elif s == last:
            source, target, b = data.at[self.cols, self.kept(chunk, last - 1)], land.at[self.cols, self.landed(chunk, last)], last
        else:
            b = 2 * last - s
            source = target = result.at[self.cols, self.kept(chunk, b)]
        return self.remote(source, target, slot, s, self.peer[b])

    def stage(self, s, chunk, slot, data, land, result, finish, adjust=None):
        last = self.last
        if s > 0:
            self.move(s - 1, chunk, slot, data, land, result).wait()
        if 0 < s <= last:
            at = self.kept(chunk, s - 1)
            data[self.cols, at] += land[self.cols, self.landed(chunk, s - 1)]
            if s == last and adjust is not None:
                adjust()
        elif s == last + 1:
            at = self.kept(chunk, last - 1)
            finish(self.cols, at, data[self.cols, at] + land[self.cols, self.landed(chunk, last)])
        if s < self.stages:
            self.move(s, chunk, slot, data, land, result).start()


class Move:
    def __init__(self, **names):
        self.names = names

    def start(self):
        pltpu.make_async_remote_copy(**self.names).start()

    def wait(self):
        pltpu.make_async_remote_copy(**self.names).wait()

    def wait_send(self):
        pltpu.make_async_remote_copy(**self.names).wait_send()

    def wait_recv(self):
        pltpu.make_async_remote_copy(**self.names).wait_recv()


class Ladder:
    def __init__(self, across, size, cols, sends, recvs, sem):
        self.size, self.half, self.cols, self.across = size, size // 2, cols, across
        self.sends, self.recvs, self.sem = sends, recvs, sem
        self.stages = 5
        me = lax.axis_index("cells")
        z, x = me // 2, me % 2
        self.inner = (z == 1) | (z == 2)
        self.side, self.rank = x, z // 2
        self.beside = me + 1 - 2 * x
        self.mate = me + 2 - 4 * (z % 2)
        self.other = me + 2 - 4 * (z // 2)

    def lane(self, chunk, start, size):
        return lanes(chunk * self.size + start, size)

    def spot(self, chunk, start, size):
        return lanes(chunk * 2 * self.size + start, size)

    def copy(self, source, target, slot, sem, peer):
        return Move(
            src_ref=source,
            dst_ref=target,
            send_sem=self.sends.at[self.sem + sem, slot],
            recv_sem=self.recvs.at[self.sem + sem, slot],
            device_id={"cells": peer},
            device_id_type=pl.DeviceIdType.MESH,
        )

    def stage(self, s, chunk, slot, data, land, result, finish):
        (self.stage_across if self.across else self.stage_along)(s, chunk, slot, data, land, result, finish)

    def stage_across(self, s, chunk, slot, data, land, result, finish):
        cols, half = self.cols, self.half
        mine = self.lane(chunk, self.side * half, half)
        away = self.lane(chunk, (1 - self.side) * half, half)
        spots = [self.spot(chunk, i * half, half) for i in range(3)]
        first = self.copy(data.at[cols, away], land.at[cols, spots[0]], slot, 0, self.beside)
        up = self.copy(data.at[cols, mine], land.at[cols, spots[1]], slot, 1, self.mate)
        swap = self.copy(data.at[cols, mine], land.at[cols, spots[2]], slot, 2, self.other)
        down = self.copy(result.at[cols, mine], result.at[cols, mine], slot, 3, self.mate)
        last = self.copy(result.at[cols, mine], result.at[cols, mine], slot, 4, self.beside)
        inner, outer = pl.when(self.inner), pl.when(jnp.logical_not(self.inner))
        if s == 0:
            first.start()
        elif s == 1:
            first.wait()
            data[cols, mine] += land[cols, spots[0]]
            outer(up.start)
        elif s == 2:
            outer(up.wait_send)

            @inner
            def _():
                up.wait_recv()
                data[cols, mine] += land[cols, spots[1]]
                swap.start()
        elif s == 3:
            @inner
            def _():
                swap.wait()
                finish(cols, mine, data[cols, mine] + land[cols, spots[2]])
                down.start()
                last.start()
        elif s == 4:
            inner(down.wait_send)

            @outer
            def _():
                down.wait_recv()
                last.start()
        else:
            last.wait()

    def stage_along(self, s, chunk, slot, data, land, result, finish):
        cols, half, size = self.cols, self.half, self.size
        whole = self.lane(chunk, 0, size)
        mine = self.lane(chunk, self.rank * half, half)
        away = self.lane(chunk, (1 - self.rank) * half, half)
        begin = self.spot(chunk, 0, size)
        spots = [self.spot(chunk, size + i * half, half) for i in range(2)]
        up = self.copy(data.at[cols, whole], land.at[cols, begin], slot, 0, self.mate)
        first = self.copy(data.at[cols, away], land.at[cols, spots[0]], slot, 1, self.other)
        swap = self.copy(data.at[cols, mine], land.at[cols, spots[1]], slot, 2, self.beside)
        last = self.copy(result.at[cols, mine], result.at[cols, mine], slot, 3, self.other)
        near = self.copy(result.at[cols, mine], result.at[cols, mine], slot, 4, self.mate)
        far = self.copy(result.at[cols, away], result.at[cols, away], slot, 5, self.mate)
        inner, outer = pl.when(self.inner), pl.when(jnp.logical_not(self.inner))
        if s == 0:
            outer(up.start)
        elif s == 1:
            outer(up.wait_send)

            @inner
            def _():
                up.wait_recv()
                data[cols, whole] += land[cols, begin]
                first.start()
        elif s == 2:
            @inner
            def _():
                first.wait()
                data[cols, mine] += land[cols, spots[0]]
                swap.start()
        elif s == 3:
            @inner
            def _():
                swap.wait()
                finish(cols, mine, data[cols, mine] + land[cols, spots[1]])
                last.start()
                near.start()
        elif s == 4:
            inner(near.wait_send)
            outer(near.wait_recv)

            @inner
            def _():
                last.wait()
                far.start()
        else:
            inner(far.wait_send)
            outer(far.wait_recv)


def body(sizes, plane, sens_hbm, obs_hbm, models_hbm, near_ref, mask_ref, out_hbm,
         sens, s_high, s_low, t_high, t_low, obs_raw, obs, part, land, weighted, grad, gland, flat, state, wide,
         pick, smooth, rim, load_sem, obs_sem, edge_sem, c_send, c_recv, d_send, d_recv, h_send, h_recv):
    n_dp, n_cells = sizes
    ndata, ncell = s_high.shape
    groups, width, _ = grad.shape
    per = LANES // width
    me = lax.axis_index("cells")
    chunks = c_send.shape[1] // (ITERS * groups)
    loads = load_sem.shape[0]
    batch = ndata // loads
    rows = ndata // chunks
    parts = ncell // plane
    prow = ncell // parts
    cell_digits, dp_digits = digits_of(n_cells), digits_of(n_dp)
    if len(cell_digits) == 3:
        straight = width - TURNED
        ways = [
            Ladder(False, rows, pl.ds(straight, TURNED), c_send, c_recv, 5),
            Ladder(True, rows, pl.ds(0, straight), c_send, c_recv, 0),
        ]
    else:
        ways = [Sum("cells", cell_digits, rows, pl.ds(0, width), c_send, c_recv)]
    cells = ways[0]
    dp = Sum("dp", dp_digits, prow, pl.ds(0, width), d_send, d_recv)
    seg = dp.size[-1]
    inner = dp.off[-1]
    side = dp.mine
    own = side * prow + inner
    units = groups * chunks
    span = STRIDE * chunks
    cell_at, dp_at = timetable(CELL_AT, cells.stages), timetable(DP_AT, dp.stages)
    behind = cell_at[cells.stages] + BACK_LAG
    delay = span - STRIDE + behind + 1
    done = delay + parts + dp_at[dp.stages]
    period = max(STRIDE * units, done)
    slots = (ITERS - 1) * period + (groups - 1) * span + done
    nn, nt = ((1,), (0,)), ((1,), (1,))

    def load(c):
        at = pl.ds(pl.multiple_of(c * batch, LANES), batch)
        return pltpu.make_async_copy(sens_hbm.at[at], sens.at[lax.rem(c, 2)], load_sem.at[c])

    def enter(p):
        at = lanes(p * LANES, LANES)
        return pltpu.make_async_copy(models_hbm.at[:, at], flat.at[:, at], edge_sem.at[p])

    def leave(p):
        at = lanes(p * LANES, LANES)
        return pltpu.make_async_copy(flat.at[:, at], out_hbm.at[:, at], edge_sem.at[p])

    def watch(p):
        at = lanes(p * LANES, LANES)
        return pltpu.make_async_copy(obs_hbm.at[:, at], obs_raw.at[:, at], obs_sem.at[p])

    pairs = groups // per
    for p in range(pairs):
        enter(p).start()
    load(0).start()
    for p in range(pairs):
        watch(p).start()
    for c in range(1, min(2, loads)):
        load(c).start()

    barrier = pltpu.get_barrier_semaphore()

    def greet(where):
        pl.semaphore_signal(barrier, inc=1, device_id=where, device_id_type=pl.DeviceIdType.MESH)

    for d in range(1, n_cells):
        greet({"cells": lax.rem(me + d, n_cells)})
    for peer in dp.peer:
        greet({"dp": peer})

    has_under, has_over = me > 0, me < n_cells - 1

    upward = side == 0
    gives = (upward & has_over) | (jnp.logical_not(upward) & has_under)
    takes = (upward & has_under) | (jnp.logical_not(upward) & has_over)

    @pl.when(jnp.logical_not(takes))
    def _():
        rim[...] = jnp.zeros_like(rim)

    for p in range(pairs):
        enter(p).wait()
        turned = flat[:, p * LANES:(p + 1) * LANES].T
        for i in range(per):
            state[0, p * per + i] = turned[i * width:(i + 1) * width]

    pl.semaphore_wait(barrier, n_cells - 1 + len(dp_digits))

    def halo(step, g, i):
        source = (1 - side) * (ncell - plane) + inner
        cols = pl.ds(pl.multiple_of(i * (width // PIECES), 8), width // PIECES)
        return pltpu.make_async_remote_copy(
            src_ref=state.at[step, g, cols, lanes(source, seg)],
            dst_ref=rim.at[step, g, cols],
            send_sem=h_send.at[step, g * PIECES + i],
            recv_sem=h_recv.at[step, g * PIECES + i],
            device_id={"cells": me + 1 - 2 * side},
            device_id_type=pl.DeviceIdType.MESH,
        )

    def border(step, g, i):
        @pl.when(gives)
        def _():
            halo(step, g, i).start()

    def predict(step, g, c):
        p, i = over(g, per)
        at = pl.ds(pl.multiple_of(c * rows, LANES), rows)
        joint = (step == 0) & (i == 0)
        top = pl.ds(pl.multiple_of(i * width, 16), width)
        low = pl.ds(pl.multiple_of(LANES + i * width, 16), width)

        @pl.when((c == 0) & joint)
        def _():
            for n in range(per):
                hi, lo = split(state[0, g + n])
                wide[p, n * width:(n + 1) * width, :] = hi
                wide[p, LANES + n * width:LANES + (n + 1) * width, :] = lo

        @pl.when((c == 0) & (step > 0))
        def _():
            hi, lo = split(state[step, g])
            wide[p, top, :] = hi
            wide[p, low, :] = lo

        @pl.when((step == 0) & (g == 0))
        def _():
            for n in range(rows // batch):
                b = c * (rows // batch) + n
                load(b).wait()
                into = pl.ds(pl.multiple_of(b * batch, LANES), batch)
                hi, lo = split(sens[lax.rem(b, 2)])
                s_high[into, :] = hi
                s_low[into, :] = lo

                @pl.when(b + 2 < loads)
                def _():
                    load(b + 2).start()

        @pl.when(joint)
        def _():
            both = dot(wide[p], s_high[at, :], nt)
            total = both[:LANES] + both[LANES:] + dot(wide[p, :LANES, :], s_low[at, :], nt)
            for n in range(per):
                part[g + n, :, at] = total[n * width:(n + 1) * width]

        @pl.when(step > 0)
        def _():
            hi = wide[p, top, :]
            both = dot(jnp.concatenate([hi, wide[p, low, :]], axis=0), t_high[:, at], nn)
            part[g, :, at] = both[:width] + both[width:] + dot(hi, t_low[:, at], nn)

    def turn(step, g, c):
        @pl.when((step == 0) & (g == 1))
        def _():
            at = pl.ds(pl.multiple_of(c * rows, LANES), rows)
            t_high[:, at] = s_high[at, :].T
            t_low[:, at] = s_low[at, :].T

    def sight(step, g, c):
        @pl.when((step == 0) & (lax.rem(g, per) == 0))
        def _():
            p = lax.div(g, per)

            @pl.when(c == 0)
            def _():
                watch(p).wait()

            at = lanes(c * rows, rows)
            turned = obs_raw[at, lanes(p * LANES, LANES)].T
            for i in range(per):
                obs[g + i, :, at] = turned[i * width:(i + 1) * width]

    def back(step, g, c):
        @pl.when(c == 0)
        def _():
            grad[g] = jnp.zeros_like(grad[g])

        at = pl.ds(pl.multiple_of(c * rows, LANES), rows)
        hi, lo = split(weighted[g, :, at])
        both = dot(jnp.concatenate([hi, lo], axis=0), s_high[at, :], nn)
        grad[g] += both[:width] + both[width:] + dot(hi, s_low[at, :], nn)

    def smooth_part(step, g, k):
        p, i = over(g, per)

        @pl.when(i == per - 1)
        def _():
            smooth_pair(step, p, k)

    def smooth_pair(step, p, k):
        @pl.when((step == 0) & (p == 0))
        def _():
            row = near_ref[pl.ds(k, 1), lanes(inner, seg)]
            chosen = lax.broadcasted_iota(jnp.int32, (plane, seg), 0) == row
            pick[k] = jnp.where(chosen, 1.0, 0.0).astype(BF16)

        mine = pl.ds(p * per, per)
        cell = state[step, mine, :, lanes(own, seg)]

        def pull(other):
            diff = other - cell
            return diff / jnp.sqrt(1.0 + diff * diff)

        @pl.when(k == 0)
        def _():
            @pl.when(gives)
            def _():
                for n in range(per):
                    for i in range(PIECES):
                        halo(step, p * per + n, i).wait_send()

            @pl.when(takes)
            def _():
                for n in range(per):
                    for i in range(PIECES):
                        halo(step, p * per + n, i).wait_recv()

            beside = state[step, mine, :, lanes((1 - side) * prow + inner, seg)]
            smooth[mine] = pull(rim[step, mine]) + pull(beside)

        both = dot(wide[p, :, lanes(side * plane, plane)], pick[k], nn)
        other = (both[:LANES] + both[LANES:]).reshape(per, width, seg)
        scale = jnp.where(k == 3, 0.05 * (1.0 - 0.75 * mask_ref[:, lanes(own, seg)].astype(F32)), 1.0)
        smooth[mine] = (smooth[mine] + pull(other)) * scale

    def at_slot(x, count, stride, act):
        step = sum((x >= i * period).astype(jnp.int32) for i in range(1, ITERS))
        g, place = over(x - step * period, span)
        index, wait = over(place, stride)

        @pl.when((x >= 0) & (g < groups) & (index < count) & (wait == 0))
        def _():
            act(step, g, index)

    def cell_stage(s, step, g, c):
        def reweight(cols, at, total):
            misfit = total - obs[g, cols, at]
            weighted[g, cols, at] = misfit / jnp.maximum(jnp.abs(misfit), 1.0)

        for way in ways:
            way.stage(s, c, step * units + g * chunks + c, part.at[g], land.at[step, g], weighted.at[g], reweight)

    def dp_stage(s, step, g, q):
        def blend():
            @pl.when(side == q)
            def _():
                grad[g, :, lanes(own, seg)] -= smooth[g]

        def update(cols, at, total):
            state[step + 1, g, :, at] = state[step, g, :, at] - 1.0 * total

        slot = (step * groups + g) * parts + q
        dp.stage(s, q, slot, grad.at[g], gland.at[step, g], state.at[step + 1, g], update, blend)

    def depart(step, g, i):
        @pl.when((step == ITERS - 1) & (lax.rem(g, per) == per - 1))
        def _():
            p = lax.div(g, per)
            rest = [state[ITERS, g - per + 1 + i] for i in range(per)]
            flat[:, lanes(p * LANES, LANES)] = jnp.concatenate(rest, axis=0).T
            leave(p).start()

    def slot(t, carry):
        for s in reversed(range(cells.stages + 1)):
            at_slot(t - cell_at[s], chunks, STRIDE, functools.partial(cell_stage, s))
        for s in reversed(range(dp.stages + 1)):
            at_slot(t - delay - dp_at[s], parts, 1, functools.partial(dp_stage, s))
        at_slot(t + 1, chunks, STRIDE, predict)
        at_slot(t - HALO_LAG, PIECES, HALO_STRIDE, border)
        at_slot(t, chunks, STRIDE, sight)
        at_slot(t + 1 - TURN_LAG, chunks, STRIDE, turn)
        at_slot(t - SMOOTH_LAG, 4, 1, smooth_part)
        at_slot(t - behind, chunks, STRIDE, back)
        at_slot(t - done + 1, 1, 1, depart)
        return carry

    lax.fori_loop(-1, slots, slot, 0)
    for p in range(pairs):
        leave(p).wait()


def invert(n_dp, n_cells, sensitivity, observed, models, neighbour_map, edge_mask):
    ndata, ncell = sensitivity.shape
    total = models.shape[1]
    width = total // GROUPS
    plane = neighbour_map.shape[1]
    nb, nd = 2 * len(digits_of(n_cells)) - 1, 2 * len(digits_of(n_dp)) - 1
    chunks = ndata // max(CHUNK, LANES * n_cells // 2)
    parts = ncell // plane
    seg = ncell // n_dp
    copies = 11 if n_cells == 8 else nb
    vmem = pl.BlockSpec(memory_space=pltpu.VMEM)
    hbm = pl.BlockSpec(memory_space=pl.ANY)
    dma = pltpu.SemaphoreType.DMA
    return pl.pallas_call(
        functools.partial(body, (n_dp, n_cells), plane),
        out_shape=jax.ShapeDtypeStruct(models.shape, F32),
        in_specs=[hbm] * 3 + [vmem] * 2,
        out_specs=hbm,
        scratch_shapes=[
            pltpu.VMEM((2, LOAD, ncell), F32),
            pltpu.VMEM((ndata, ncell), BF16),
            pltpu.VMEM((ndata, ncell), BF16),
            pltpu.VMEM((ncell, ndata), BF16),
            pltpu.VMEM((ncell, ndata), BF16),
            pltpu.VMEM((ndata, total), F32),
            pltpu.VMEM((GROUPS, width, ndata), F32),
            pltpu.VMEM((GROUPS, width, ndata), F32),
            pltpu.VMEM((ITERS, GROUPS, width, 2 * ndata), F32),
            pltpu.VMEM((GROUPS, width, ndata), F32),
            pltpu.VMEM((GROUPS, width, ncell), F32),
            pltpu.VMEM((ITERS, GROUPS, width, ncell), F32),
            pltpu.VMEM((ncell, total), F32),
            pltpu.VMEM((ITERS + 1, GROUPS, width, ncell), F32),
            pltpu.VMEM((GROUPS * width // LANES, 2 * LANES, ncell), BF16),
            pltpu.VMEM((4, plane, seg), BF16),
            pltpu.VMEM((GROUPS, width, seg), F32),
            pltpu.VMEM((ITERS, GROUPS, width, seg), F32),
            dma((ndata // LOAD,)),
            dma((GROUPS * width // LANES,)),
            dma((GROUPS * width // LANES,)),
            dma((copies, ITERS * GROUPS * chunks)),
            dma((copies, ITERS * GROUPS * chunks)),
            dma((nd, ITERS * GROUPS * parts)),
            dma((nd, ITERS * GROUPS * parts)),
            dma((ITERS, GROUPS * PIECES)),
            dma((ITERS, GROUPS * PIECES)),
        ],
        compiler_params=pltpu.CompilerParams(
            collective_id=0, has_side_effects=True, vmem_limit_bytes=67043328
        ),
        name="invert",
    )(sensitivity, observed, models, neighbour_map, edge_mask[None, :])


def solution(mesh):
    return jax.shard_map(
        functools.partial(invert, mesh.shape["dp"], mesh.shape["cells"]),
        mesh=mesh,
        in_specs=(P("dp", "cells"), P("dp", None), P("cells", None), P(), P("cells")),
        out_specs=P("cells", None),
        check_vma=False,
    )
```

```python
import functools

import jax
import jax.numpy as jnp
from jax import lax
from jax.experimental import pallas as pl
from jax.experimental.pallas import tpu as pltpu
from jax.sharding import PartitionSpec as P

ITERS = 2
CHUNK = 512
LOAD = 256
TURN_LAG = 0
GROUPS = 4
CELL_AT = (0, 4, 7, 10, 13, 16)
BACK_LAG = 0
DP_AT = (0, 2, 5, 7)
PIECES = 4
HALO_LAG = 0
HALO_STRIDE = 2
SMOOTH_LAG = 11
STRIDE = 2
TURNED = 32
LANES = 128
F32 = jnp.float32
BF16 = jnp.bfloat16


def split(x):
    hi = x.astype(BF16)
    return hi, (x - hi.astype(F32)).astype(BF16)


def digits_of(count):
    digits = []
    while count > 1:
        digits.append(2)
        count //= 2
    return digits


def dot(a, b, dims):
    return lax.dot_general(a, b, (dims, ((), ())), preferred_element_type=F32)


def over(x, n):
    if n & (n - 1):
        return lax.div(x, n), lax.rem(x, n)
    return lax.shift_right_logical(x, n.bit_length() - 1), lax.bitwise_and(x, n - 1)


def timetable(times, stages):
    times = list(times)
    while len(times) <= stages:
        times.append(times[-1] + 3)
    return times


def lanes(start, size):
    return pl.ds(pl.multiple_of(start, LANES), size)


class Sum:
    def __init__(self, axis, digits, size, cols, sends, recvs):
        strides = [1]
        for base in digits[:-1]:
            strides.append(strides[-1] * base)
        self.axis, self.cols, self.pitch = axis, cols, size
        self.sends, self.recvs = sends, recvs
        self.last = len(digits) - 1
        self.stages = 2 * self.last + 1
        me = lax.axis_index(axis)
        self.peer, self.away, self.off, self.size = [], [], [0], [size]
        for b in range(len(digits)):
            stride = strides[b]
            mine = (me // stride) % 2
            self.peer.append(me + (1 - 2 * mine) * stride)
            self.mine = mine
            if b < self.last:
                piece = self.size[b] // 2
                self.away.append(self.off[b] + (1 - mine) * piece)
                self.off.append(self.off[b] + mine * piece)
                self.size.append(piece)

    def kept(self, chunk, b):
        return lanes(chunk * self.pitch + self.off[b + 1], self.size[b + 1])

    def landed(self, chunk, b):
        size = self.size[min(b + 1, self.last)]
        return lanes(chunk * self.pitch + self.pitch - self.size[b], size)

    def remote(self, source, target, slot, sem, peer):
        return pltpu.make_async_remote_copy(
            src_ref=source,
            dst_ref=target,
            send_sem=self.sends.at[sem, slot],
            recv_sem=self.recvs.at[sem, slot],
            device_id={self.axis: peer},
            device_id_type=pl.DeviceIdType.MESH,
        )

    def move(self, s, chunk, slot, data, land, result):
        last = self.last
        if s < last:
            away = lanes(chunk * self.pitch + self.away[s], self.size[s + 1])
            source, target, b = data.at[self.cols, away], land.at[self.cols, self.landed(chunk, s)], s
        elif s == last:
            source, target, b = data.at[self.cols, self.kept(chunk, last - 1)], land.at[self.cols, self.landed(chunk, last)], last
        else:
            b = 2 * last - s
            source = target = result.at[self.cols, self.kept(chunk, b)]
        return self.remote(source, target, slot, s, self.peer[b])

    def stage(self, s, chunk, slot, data, land, result, finish, adjust=None):
        last = self.last
        if s > 0:
            self.move(s - 1, chunk, slot, data, land, result).wait()
        if 0 < s <= last:
            at = self.kept(chunk, s - 1)
            data[self.cols, at] += land[self.cols, self.landed(chunk, s - 1)]
            if s == last and adjust is not None:
                adjust()
        elif s == last + 1:
            at = self.kept(chunk, last - 1)
            finish(self.cols, at, data[self.cols, at] + land[self.cols, self.landed(chunk, last)])
        if s < self.stages:
            self.move(s, chunk, slot, data, land, result).start()


class Move:
    def __init__(self, **names):
        self.names = names

    def start(self):
        pltpu.make_async_remote_copy(**self.names).start()

    def wait(self):
        pltpu.make_async_remote_copy(**self.names).wait()

    def wait_send(self):
        pltpu.make_async_remote_copy(**self.names).wait_send()

    def wait_recv(self):
        pltpu.make_async_remote_copy(**self.names).wait_recv()


class Ladder:
    def __init__(self, across, size, cols, sends, recvs, sem):
        self.size, self.half, self.cols, self.across = size, size // 2, cols, across
        self.sends, self.recvs, self.sem = sends, recvs, sem
        self.stages = 5
        me = lax.axis_index("cells")
        z, x = me // 2, me % 2
        self.inner = (z == 1) | (z == 2)
        self.side, self.rank = x, z // 2
        self.beside = me + 1 - 2 * x
        self.mate = me + 2 - 4 * (z % 2)
        self.other = me + 2 - 4 * (z // 2)

    def lane(self, chunk, start, size):
        return lanes(chunk * self.size + start, size)

    def spot(self, chunk, start, size):
        return lanes(chunk * 2 * self.size + start, size)

    def copy(self, source, target, slot, sem, peer):
        return Move(
            src_ref=source,
            dst_ref=target,
            send_sem=self.sends.at[self.sem + sem, slot],
            recv_sem=self.recvs.at[self.sem + sem, slot],
            device_id={"cells": peer},
            device_id_type=pl.DeviceIdType.MESH,
        )

    def stage(self, s, chunk, slot, data, land, result, finish):
        (self.stage_across if self.across else self.stage_along)(s, chunk, slot, data, land, result, finish)

    def stage_across(self, s, chunk, slot, data, land, result, finish):
        cols, half = self.cols, self.half
        mine = self.lane(chunk, self.side * half, half)
        away = self.lane(chunk, (1 - self.side) * half, half)
        spots = [self.spot(chunk, i * half, half) for i in range(3)]
        first = self.copy(data.at[cols, away], land.at[cols, spots[0]], slot, 0, self.beside)
        up = self.copy(data.at[cols, mine], land.at[cols, spots[1]], slot, 1, self.mate)
        swap = self.copy(data.at[cols, mine], land.at[cols, spots[2]], slot, 2, self.other)
        down = self.copy(result.at[cols, mine], result.at[cols, mine], slot, 3, self.mate)
        last = self.copy(result.at[cols, mine], result.at[cols, mine], slot, 4, self.beside)
        inner, outer = pl.when(self.inner), pl.when(jnp.logical_not(self.inner))
        if s == 0:
            first.start()
        elif s == 1:
            first.wait()
            data[cols, mine] += land[cols, spots[0]]
            outer(up.start)
        elif s == 2:
            outer(up.wait_send)

            @inner
            def _():
                up.wait_recv()
                data[cols, mine] += land[cols, spots[1]]
                swap.start()
        elif s == 3:
            @inner
            def _():
                swap.wait()
                finish(cols, mine, data[cols, mine] + land[cols, spots[2]])
                down.start()
                last.start()
        elif s == 4:
            inner(down.wait_send)

            @outer
            def _():
                down.wait_recv()
                last.start()
        else:
            last.wait()

    def stage_along(self, s, chunk, slot, data, land, result, finish):
        cols, half, size = self.cols, self.half, self.size
        whole = self.lane(chunk, 0, size)
        mine = self.lane(chunk, self.rank * half, half)
        away = self.lane(chunk, (1 - self.rank) * half, half)
        begin = self.spot(chunk, 0, size)
        spots = [self.spot(chunk, size + i * half, half) for i in range(2)]
        up = self.copy(data.at[cols, whole], land.at[cols, begin], slot, 0, self.mate)
        first = self.copy(data.at[cols, away], land.at[cols, spots[0]], slot, 1, self.other)
        swap = self.copy(data.at[cols, mine], land.at[cols, spots[1]], slot, 2, self.beside)
        last = self.copy(result.at[cols, mine], result.at[cols, mine], slot, 3, self.other)
        near = self.copy(result.at[cols, mine], result.at[cols, mine], slot, 4, self.mate)
        far = self.copy(result.at[cols, away], result.at[cols, away], slot, 5, self.mate)
        inner, outer = pl.when(self.inner), pl.when(jnp.logical_not(self.inner))
        if s == 0:
            outer(up.start)
        elif s == 1:
            outer(up.wait_send)

            @inner
            def _():
                up.wait_recv()
                data[cols, whole] += land[cols, begin]
                first.start()
        elif s == 2:
            @inner
            def _():
                first.wait()
                data[cols, mine] += land[cols, spots[0]]
                swap.start()
        elif s == 3:
            @inner
            def _():
                swap.wait()
                finish(cols, mine, data[cols, mine] + land[cols, spots[1]])
                last.start()
                near.start()
        elif s == 4:
            inner(near.wait_send)
            outer(near.wait_recv)

            @inner
            def _():
                last.wait()
                far.start()
        else:
            inner(far.wait_send)
            outer(far.wait_recv)


def body(sizes, plane, sens_hbm, obs_hbm, models_hbm, near_ref, mask_ref, out_hbm,
         sens, s_high, s_low, t_high, t_low, obs_raw, obs, part, land, weighted, grad, gland, flat, state, wide,
         pick, smooth, rim, load_sem, obs_sem, edge_sem, c_send, c_recv, d_send, d_recv, h_send, h_recv):
    n_dp, n_cells = sizes
    ndata, ncell = s_high.shape
    groups, width, _ = grad.shape
    per = LANES // width
    me = lax.axis_index("cells")
    chunks = c_send.shape[1] // (ITERS * groups)
    loads = load_sem.shape[0]
    batch = ndata // loads
    rows = ndata // chunks
    parts = ncell // plane
    prow = ncell // parts
    cell_digits, dp_digits = digits_of(n_cells), digits_of(n_dp)
    if len(cell_digits) == 3:
        straight = width - TURNED
        ways = [
            Ladder(False, rows, pl.ds(straight, TURNED), c_send, c_recv, 5),
            Ladder(True, rows, pl.ds(0, straight), c_send, c_recv, 0),
        ]
    else:
        ways = [Sum("cells", cell_digits, rows, pl.ds(0, width), c_send, c_recv)]
    cells = ways[0]
    dp = Sum("dp", dp_digits, prow, pl.ds(0, width), d_send, d_recv)
    seg = dp.size[-1]
    inner = dp.off[-1]
    side = dp.mine
    own = side * prow + inner
    units = groups * chunks
    span = STRIDE * chunks
    cell_at, dp_at = timetable(CELL_AT, cells.stages), timetable(DP_AT, dp.stages)
    behind = cell_at[cells.stages] + BACK_LAG
    delay = span - STRIDE + behind + 1
    done = delay + parts + dp_at[dp.stages]
    period = max(STRIDE * units, done)
    slots = (ITERS - 1) * period + (groups - 1) * span + done
    nn, nt = ((1,), (0,)), ((1,), (1,))

    def load(c):
        at = pl.ds(pl.multiple_of(c * batch, LANES), batch)
        return pltpu.make_async_copy(sens_hbm.at[at], sens.at[lax.rem(c, 2)], load_sem.at[c])

    def enter(p):
        at = lanes(p * LANES, LANES)
        return pltpu.make_async_copy(models_hbm.at[:, at], flat.at[:, at], edge_sem.at[p])

    def leave(p):
        at = lanes(p * LANES, LANES)
        return pltpu.make_async_copy(flat.at[:, at], out_hbm.at[:, at], edge_sem.at[p])

    def watch(p):
        at = lanes(p * LANES, LANES)
        return pltpu.make_async_copy(obs_hbm.at[:, at], obs_raw.at[:, at], obs_sem.at[p])

    pairs = groups // per
    for p in range(pairs):
        enter(p).start()
    load(0).start()
    for p in range(pairs):
        watch(p).start()
    for c in range(1, min(2, loads)):
        load(c).start()

    barrier = pltpu.get_barrier_semaphore()

    def greet(where):
        pl.semaphore_signal(barrier, inc=1, device_id=where, device_id_type=pl.DeviceIdType.MESH)

    for d in range(1, n_cells):
        greet({"cells": lax.rem(me + d, n_cells)})
    for peer in dp.peer:
        greet({"dp": peer})

    has_under, has_over = me > 0, me < n_cells - 1

    upward = side == 0
    gives = (upward & has_over) | (jnp.logical_not(upward) & has_under)
    takes = (upward & has_under) | (jnp.logical_not(upward) & has_over)

    @pl.when(jnp.logical_not(takes))
    def _():
        rim[...] = jnp.zeros_like(rim)

    for p in range(pairs):
        enter(p).wait()
        turned = flat[:, p * LANES:(p + 1) * LANES].T
        for i in range(per):
            state[0, p * per + i] = turned[i * width:(i + 1) * width]

    pl.semaphore_wait(barrier, n_cells - 1 + len(dp_digits))

    def halo(step, g, i):
        source = (1 - side) * (ncell - plane) + inner
        cols = pl.ds(pl.multiple_of(i * (width // PIECES), 8), width // PIECES)
        return pltpu.make_async_remote_copy(
            src_ref=state.at[step, g, cols, lanes(source, seg)],
            dst_ref=rim.at[step, g, cols],
            send_sem=h_send.at[step, g * PIECES + i],
            recv_sem=h_recv.at[step, g * PIECES + i],
            device_id={"cells": me + 1 - 2 * side},
            device_id_type=pl.DeviceIdType.MESH,
        )

    def border(step, g, i):
        @pl.when(gives)
        def _():
            halo(step, g, i).start()

    def predict(step, g, c):
        p, i = over(g, per)
        at = pl.ds(pl.multiple_of(c * rows, LANES), rows)
        joint = (step == 0) & (i == 0)
        top = pl.ds(pl.multiple_of(i * width, 16), width)
        low = pl.ds(pl.multiple_of(LANES + i * width, 16), width)

        @pl.when((c == 0) & joint)
        def _():
            for n in range(per):
                hi, lo = split(state[0, g + n])
                wide[p, n * width:(n + 1) * width, :] = hi
                wide[p, LANES + n * width:LANES + (n + 1) * width, :] = lo

        @pl.when((c == 0) & (step > 0))
        def _():
            hi, lo = split(state[step, g])
            wide[p, top, :] = hi
            wide[p, low, :] = lo

        @pl.when((step == 0) & (g == 0))
        def _():
            for n in range(rows // batch):
                b = c * (rows // batch) + n
                load(b).wait()
                into = pl.ds(pl.multiple_of(b * batch, LANES), batch)
                hi, lo = split(sens[lax.rem(b, 2)])
                s_high[into, :] = hi
                s_low[into, :] = lo

                @pl.when(b + 2 < loads)
                def _():
                    load(b + 2).start()

        @pl.when(joint)
        def _():
            both = dot(wide[p], s_high[at, :], nt)
            total = both[:LANES] + both[LANES:] + dot(wide[p, :LANES, :], s_low[at, :], nt)
            for n in range(per):
                part[g + n, :, at] = total[n * width:(n + 1) * width]

        @pl.when(step > 0)
        def _():
            hi = wide[p, top, :]
            both = dot(jnp.concatenate([hi, wide[p, low, :]], axis=0), t_high[:, at], nn)
            part[g, :, at] = both[:width] + both[width:] + dot(hi, t_low[:, at], nn)

    def turn(step, g, c):
        @pl.when((step == 0) & (g == 1))
        def _():
            at = pl.ds(pl.multiple_of(c * rows, LANES), rows)
            t_high[:, at] = s_high[at, :].T
            t_low[:, at] = s_low[at, :].T

    def sight(step, g, c):
        @pl.when((step == 0) & (lax.rem(g, per) == 0))
        def _():
            p = lax.div(g, per)

            @pl.when(c == 0)
            def _():
                watch(p).wait()

            at = lanes(c * rows, rows)
            turned = obs_raw[at, lanes(p * LANES, LANES)].T
            for i in range(per):
                obs[g + i, :, at] = turned[i * width:(i + 1) * width]

    def back(step, g, c):
        @pl.when(c == 0)
        def _():
            grad[g] = jnp.zeros_like(grad[g])

        at = pl.ds(pl.multiple_of(c * rows, LANES), rows)
        hi, lo = split(weighted[g, :, at])
        both = dot(jnp.concatenate([hi, lo], axis=0), s_high[at, :], nn)
        grad[g] += both[:width] + both[width:] + dot(hi, s_low[at, :], nn)

    def smooth_part(step, g, k):
        p, i = over(g, per)

        @pl.when(i == per - 1)
        def _():
            smooth_pair(step, p, k)

    def smooth_pair(step, p, k):
        @pl.when((step == 0) & (p == 0))
        def _():
            row = near_ref[pl.ds(k, 1), lanes(inner, seg)]
            chosen = lax.broadcasted_iota(jnp.int32, (plane, seg), 0) == row
            pick[k] = jnp.where(chosen, 1.0, 0.0).astype(BF16)

        mine = pl.ds(p * per, per)
        cell = state[step, mine, :, lanes(own, seg)]

        def pull(other):
            diff = other - cell
            return diff / jnp.sqrt(1.0 + diff * diff)

        @pl.when(k == 0)
        def _():
            @pl.when(gives)
            def _():
                for n in range(per):
                    for i in range(PIECES):
                        halo(step, p * per + n, i).wait_send()

            @pl.when(takes)
            def _():
                for n in range(per):
                    for i in range(PIECES):
                        halo(step, p * per + n, i).wait_recv()

            beside = state[step, mine, :, lanes((1 - side) * prow + inner, seg)]
            smooth[mine] = pull(rim[step, mine]) + pull(beside)

        both = dot(wide[p, :, lanes(side * plane, plane)], pick[k], nn)
        other = (both[:LANES] + both[LANES:]).reshape(per, width, seg)
        scale = jnp.where(k == 3, 0.05 * (1.0 - 0.75 * mask_ref[:, lanes(own, seg)].astype(F32)), 1.0)
        smooth[mine] = (smooth[mine] + pull(other)) * scale

    def at_slot(x, count, stride, act):
        step = sum((x >= i * period).astype(jnp.int32) for i in range(1, ITERS))
        g, place = over(x - step * period, span)
        index, wait = over(place, stride)

        @pl.when((x >= 0) & (g < groups) & (index < count) & (wait == 0))
        def _():
            act(step, g, index)

    def cell_stage(s, step, g, c):
        def reweight(cols, at, total):
            misfit = total - obs[g, cols, at]
            weighted[g, cols, at] = misfit / jnp.maximum(jnp.abs(misfit), 1.0)

        for way in ways:
            way.stage(s, c, step * units + g * chunks + c, part.at[g], land.at[step, g], weighted.at[g], reweight)

    def dp_stage(s, step, g, q):
        def blend():
            @pl.when(side == q)
            def _():
                grad[g, :, lanes(own, seg)] -= smooth[g]

        def update(cols, at, total):
            state[step + 1, g, :, at] = state[step, g, :, at] - 1.0 * total

        slot = (step * groups + g) * parts + q
        dp.stage(s, q, slot, grad.at[g], gland.at[step, g], state.at[step + 1, g], update, blend)

    def depart(step, g, i):
        @pl.when((step == ITERS - 1) & (lax.rem(g, per) == per - 1))
        def _():
            p = lax.div(g, per)
            rest = [state[ITERS, g - per + 1 + i] for i in range(per)]
            flat[:, lanes(p * LANES, LANES)] = jnp.concatenate(rest, axis=0).T
            leave(p).start()

    def slot(t, carry):
        for s in reversed(range(cells.stages + 1)):
            at_slot(t - cell_at[s], chunks, STRIDE, functools.partial(cell_stage, s))
        for s in reversed(range(dp.stages + 1)):
            at_slot(t - delay - dp_at[s], parts, 1, functools.partial(dp_stage, s))
        at_slot(t + 1, chunks, STRIDE, predict)
        at_slot(t - HALO_LAG, PIECES, HALO_STRIDE, border)
        at_slot(t, chunks, STRIDE, sight)
        at_slot(t + 1 - TURN_LAG, chunks, STRIDE, turn)
        at_slot(t - SMOOTH_LAG, 4, 1, smooth_part)
        at_slot(t - behind, chunks, STRIDE, back)
        at_slot(t - done + 1, 1, 1, depart)
        return carry

    lax.fori_loop(-1, slots, slot, 0)
    for p in range(pairs):
        leave(p).wait()


def invert(n_dp, n_cells, sensitivity, observed, models, neighbour_map, edge_mask):
    ndata, ncell = sensitivity.shape
    total = models.shape[1]
    width = total // GROUPS
    plane = neighbour_map.shape[1]
    nb, nd = 2 * len(digits_of(n_cells)) - 1, 2 * len(digits_of(n_dp)) - 1
    chunks = ndata // max(CHUNK, LANES * n_cells // 2)
    parts = ncell // plane
    seg = ncell // n_dp
    copies = 11 if n_cells == 8 else nb
    vmem = pl.BlockSpec(memory_space=pltpu.VMEM)
    hbm = pl.BlockSpec(memory_space=pl.ANY)
    dma = pltpu.SemaphoreType.DMA
    return pl.pallas_call(
        functools.partial(body, (n_dp, n_cells), plane),
        out_shape=jax.ShapeDtypeStruct(models.shape, F32),
        in_specs=[hbm] * 3 + [vmem] * 2,
        out_specs=hbm,
        scratch_shapes=[
            pltpu.VMEM((2, LOAD, ncell), F32),
            pltpu.VMEM((ndata, ncell), BF16),
            pltpu.VMEM((ndata, ncell), BF16),
            pltpu.VMEM((ncell, ndata), BF16),
            pltpu.VMEM((ncell, ndata), BF16),
            pltpu.VMEM((ndata, total), F32),
            pltpu.VMEM((GROUPS, width, ndata), F32),
            pltpu.VMEM((GROUPS, width, ndata), F32),
            pltpu.VMEM((ITERS, GROUPS, width, 2 * ndata), F32),
            pltpu.VMEM((GROUPS, width, ndata), F32),
            pltpu.VMEM((GROUPS, width, ncell), F32),
            pltpu.VMEM((ITERS, GROUPS, width, ncell), F32),
            pltpu.VMEM((ncell, total), F32),
            pltpu.VMEM((ITERS + 1, GROUPS, width, ncell), F32),
            pltpu.VMEM((GROUPS * width // LANES, 2 * LANES, ncell), BF16),
            pltpu.VMEM((4, plane, seg), BF16),
            pltpu.VMEM((GROUPS, width, seg), F32),
            pltpu.VMEM((ITERS, GROUPS, width, seg), F32),
            dma((ndata // LOAD,)),
            dma((GROUPS * width // LANES,)),
            dma((GROUPS * width // LANES,)),
            dma((copies, ITERS * GROUPS * chunks)),
            dma((copies, ITERS * GROUPS * chunks)),
            dma((nd, ITERS * GROUPS * parts)),
            dma((nd, ITERS * GROUPS * parts)),
            dma((ITERS, GROUPS * PIECES)),
            dma((ITERS, GROUPS * PIECES)),
        ],
        compiler_params=pltpu.CompilerParams(
            collective_id=0, has_side_effects=True, vmem_limit_bytes=67043328
        ),
        name="invert",
    )(sensitivity, observed, models, neighbour_map, edge_mask[None, :])


def solution(mesh):
    return jax.shard_map(
        functools.partial(invert, mesh.shape["dp"], mesh.shape["cells"]),
        mesh=mesh,
        in_specs=(P("dp", "cells"), P("dp", None), P("cells", None), P(), P("cells")),
        out_specs=P("cells", None),
        check_vma=False,
    )
```

```python
import functools

import jax
import jax.numpy as jnp
from jax import lax
from jax.experimental import pallas as pl
from jax.experimental.pallas import tpu as pltpu
from jax.sharding import PartitionSpec as P

ITERS = 2
CHUNK = 512
LOAD = 256
TURN_LAG = 0
GROUPS = 4
CELL_AT = (0, 4, 7, 10, 13, 16)
BACK_LAG = 0
DP_AT = (0, 2, 5, 7)
PIECES = 4
HALO_LAG = 0
HALO_STRIDE = 2
SMOOTH_LAG = 11
STRIDE = 2
TURNED = 32
LANES = 128
F32 = jnp.float32
BF16 = jnp.bfloat16


def split(x):
    hi = x.astype(BF16)
    return hi, (x - hi.astype(F32)).astype(BF16)


def digits_of(count):
    digits = []
    while count > 1:
        digits.append(2)
        count //= 2
    return digits


def dot(a, b, dims):
    return lax.dot_general(a, b, (dims, ((), ())), preferred_element_type=F32)


def over(x, n):
    if n & (n - 1):
        return lax.div(x, n), lax.rem(x, n)
    return lax.shift_right_logical(x, n.bit_length() - 1), lax.bitwise_and(x, n - 1)


def timetable(times, stages):
    times = list(times)
    while len(times) <= stages:
        times.append(times[-1] + 3)
    return times


def lanes(start, size):
    return pl.ds(pl.multiple_of(start, LANES), size)


class Sum:
    def __init__(self, axis, digits, size, cols, sends, recvs):
        strides = [1]
        for base in digits[:-1]:
            strides.append(strides[-1] * base)
        self.axis, self.cols, self.pitch = axis, cols, size
        self.sends, self.recvs = sends, recvs
        self.last = len(digits) - 1
        self.stages = 2 * self.last + 1
        me = lax.axis_index(axis)
        self.peer, self.away, self.off, self.size = [], [], [0], [size]
        for b in range(len(digits)):
            stride = strides[b]
            mine = (me // stride) % 2
            self.peer.append(me + (1 - 2 * mine) * stride)
            self.mine = mine
            if b < self.last:
                piece = self.size[b] // 2
                self.away.append(self.off[b] + (1 - mine) * piece)
                self.off.append(self.off[b] + mine * piece)
                self.size.append(piece)

    def kept(self, chunk, b):
        return lanes(chunk * self.pitch + self.off[b + 1], self.size[b + 1])

    def landed(self, chunk, b):
        size = self.size[min(b + 1, self.last)]
        return lanes(chunk * self.pitch + self.pitch - self.size[b], size)

    def remote(self, source, target, slot, sem, peer):
        return pltpu.make_async_remote_copy(
            src_ref=source,
            dst_ref=target,
            send_sem=self.sends.at[sem, slot],
            recv_sem=self.recvs.at[sem, slot],
            device_id={self.axis: peer},
            device_id_type=pl.DeviceIdType.MESH,
        )

    def move(self, s, chunk, slot, data, land, result):
        last = self.last
        if s < last:
            away = lanes(chunk * self.pitch + self.away[s], self.size[s + 1])
            source, target, b = data.at[self.cols, away], land.at[self.cols, self.landed(chunk, s)], s
        elif s == last:
            source, target, b = data.at[self.cols, self.kept(chunk, last - 1)], land.at[self.cols, self.landed(chunk, last)], last
        else:
            b = 2 * last - s
            source = target = result.at[self.cols, self.kept(chunk, b)]
        return self.remote(source, target, slot, s, self.peer[b])

    def stage(self, s, chunk, slot, data, land, result, finish, adjust=None):
        last = self.last
        if s > 0:
            self.move(s - 1, chunk, slot, data, land, result).wait()
        if 0 < s <= last:
            at = self.kept(chunk, s - 1)
            data[self.cols, at] += land[self.cols, self.landed(chunk, s - 1)]
            if s == last and adjust is not None:
                adjust()
        elif s == last + 1:
            at = self.kept(chunk, last - 1)
            finish(self.cols, at, data[self.cols, at] + land[self.cols, self.landed(chunk, last)])
        if s < self.stages:
            self.move(s, chunk, slot, data, land, result).start()


class Move:
    def __init__(self, **names):
        self.names = names

    def start(self):
        pltpu.make_async_remote_copy(**self.names).start()

    def wait(self):
        pltpu.make_async_remote_copy(**self.names).wait()

    def wait_send(self):
        pltpu.make_async_remote_copy(**self.names).wait_send()

    def wait_recv(self):
        pltpu.make_async_remote_copy(**self.names).wait_recv()


class Ladder:
    def __init__(self, across, size, cols, sends, recvs, sem):
        self.size, self.half, self.cols, self.across = size, size // 2, cols, across
        self.sends, self.recvs, self.sem = sends, recvs, sem
        self.stages = 5
        me = lax.axis_index("cells")
        z, x = me // 2, me % 2
        self.inner = (z == 1) | (z == 2)
        self.side, self.rank = x, z // 2
        self.beside = me + 1 - 2 * x
        self.mate = me + 2 - 4 * (z % 2)
        self.other = me + 2 - 4 * (z // 2)

    def lane(self, chunk, start, size):
        return lanes(chunk * self.size + start, size)

    def spot(self, chunk, start, size):
        return lanes(chunk * 2 * self.size + start, size)

    def copy(self, source, target, slot, sem, peer):
        return Move(
            src_ref=source,
            dst_ref=target,
            send_sem=self.sends.at[self.sem + sem, slot],
            recv_sem=self.recvs.at[self.sem + sem, slot],
            device_id={"cells": peer},
            device_id_type=pl.DeviceIdType.MESH,
        )

    def stage(self, s, chunk, slot, data, land, result, finish):
        (self.stage_across if self.across else self.stage_along)(s, chunk, slot, data, land, result, finish)

    def stage_across(self, s, chunk, slot, data, land, result, finish):
        cols, half = self.cols, self.half
        mine = self.lane(chunk, self.side * half, half)
        away = self.lane(chunk, (1 - self.side) * half, half)
        spots = [self.spot(chunk, i * half, half) for i in range(3)]
        first = self.copy(data.at[cols, away], land.at[cols, spots[0]], slot, 0, self.beside)
        up = self.copy(data.at[cols, mine], land.at[cols, spots[1]], slot, 1, self.mate)
        swap = self.copy(data.at[cols, mine], land.at[cols, spots[2]], slot, 2, self.other)
        down = self.copy(result.at[cols, mine], result.at[cols, mine], slot, 3, self.mate)
        last = self.copy(result.at[cols, mine], result.at[cols, mine], slot, 4, self.beside)
        inner, outer = pl.when(self.inner), pl.when(jnp.logical_not(self.inner))
        if s == 0:
            first.start()
        elif s == 1:
            first.wait()
            data[cols, mine] += land[cols, spots[0]]
            outer(up.start)
        elif s == 2:
            outer(up.wait_send)

            @inner
            def _():
                up.wait_recv()
                data[cols, mine] += land[cols, spots[1]]
                swap.start()
        elif s == 3:
            @inner
            def _():
                swap.wait()
                finish(cols, mine, data[cols, mine] + land[cols, spots[2]])
                down.start()
                last.start()
        elif s == 4:
            inner(down.wait_send)

            @outer
            def _():
                down.wait_recv()
                last.start()
        else:
            last.wait()

    def stage_along(self, s, chunk, slot, data, land, result, finish):
        cols, half, size = self.cols, self.half, self.size
        whole = self.lane(chunk, 0, size)
        mine = self.lane(chunk, self.rank * half, half)
        away = self.lane(chunk, (1 - self.rank) * half, half)
        begin = self.spot(chunk, 0, size)
        spots = [self.spot(chunk, size + i * half, half) for i in range(2)]
        up = self.copy(data.at[cols, whole], land.at[cols, begin], slot, 0, self.mate)
        first = self.copy(data.at[cols, away], land.at[cols, spots[0]], slot, 1, self.other)
        swap = self.copy(data.at[cols, mine], land.at[cols, spots[1]], slot, 2, self.beside)
        last = self.copy(result.at[cols, mine], result.at[cols, mine], slot, 3, self.other)
        near = self.copy(result.at[cols, mine], result.at[cols, mine], slot, 4, self.mate)
        far = self.copy(result.at[cols, away], result.at[cols, away], slot, 5, self.mate)
        inner, outer = pl.when(self.inner), pl.when(jnp.logical_not(self.inner))
        if s == 0:
            outer(up.start)
        elif s == 1:
            outer(up.wait_send)

            @inner
            def _():
                up.wait_recv()
                data[cols, whole] += land[cols, begin]
                first.start()
        elif s == 2:
            @inner
            def _():
                first.wait()
                data[cols, mine] += land[cols, spots[0]]
                swap.start()
        elif s == 3:
            @inner
            def _():
                swap.wait()
                finish(cols, mine, data[cols, mine] + land[cols, spots[1]])
                last.start()
                near.start()
        elif s == 4:
            inner(near.wait_send)
            outer(near.wait_recv)

            @inner
            def _():
                last.wait()
                far.start()
        else:
            inner(far.wait_send)
            outer(far.wait_recv)


def body(sizes, plane, sens_hbm, obs_hbm, models_hbm, near_ref, mask_ref, out_hbm,
         sens, s_high, s_low, t_high, t_low, obs_raw, obs, part, land, weighted, grad, gland, flat, state, wide,
         pick, smooth, rim, load_sem, obs_sem, edge_sem, c_send, c_recv, d_send, d_recv, h_send, h_recv):
    n_dp, n_cells = sizes
    ndata, ncell = s_high.shape
    groups, width, _ = grad.shape
    per = LANES // width
    me = lax.axis_index("cells")
    chunks = c_send.shape[1] // (ITERS * groups)
    loads = load_sem.shape[0]
    batch = ndata // loads
    rows = ndata // chunks
    parts = ncell // plane
    prow = ncell // parts
    cell_digits, dp_digits = digits_of(n_cells), digits_of(n_dp)
    if len(cell_digits) == 3:
        straight = width - TURNED
        ways = [
            Ladder(False, rows, pl.ds(straight, TURNED), c_send, c_recv, 5),
            Ladder(True, rows, pl.ds(0, straight), c_send, c_recv, 0),
        ]
    else:
        ways = [Sum("cells", cell_digits, rows, pl.ds(0, width), c_send, c_recv)]
    cells = ways[0]
    dp = Sum("dp", dp_digits, prow, pl.ds(0, width), d_send, d_recv)
    seg = dp.size[-1]
    inner = dp.off[-1]
    side = dp.mine
    own = side * prow + inner
    units = groups * chunks
    span = STRIDE * chunks
    cell_at, dp_at = timetable(CELL_AT, cells.stages), timetable(DP_AT, dp.stages)
    behind = cell_at[cells.stages] + BACK_LAG
    delay = span - STRIDE + behind + 1
    done = delay + parts + dp_at[dp.stages]
    period = max(STRIDE * units, done)
    slots = (ITERS - 1) * period + (groups - 1) * span + done
    nn, nt = ((1,), (0,)), ((1,), (1,))

    def load(c):
        at = pl.ds(pl.multiple_of(c * batch, LANES), batch)
        return pltpu.make_async_copy(sens_hbm.at[at], sens.at[lax.rem(c, 2)], load_sem.at[c])

    def enter(p):
        at = lanes(p * LANES, LANES)
        return pltpu.make_async_copy(models_hbm.at[:, at], flat.at[:, at], edge_sem.at[p])

    def leave(p):
        at = lanes(p * LANES, LANES)
        return pltpu.make_async_copy(flat.at[:, at], out_hbm.at[:, at], edge_sem.at[p])

    def watch(p):
        at = lanes(p * LANES, LANES)
        return pltpu.make_async_copy(obs_hbm.at[:, at], obs_raw.at[:, at], obs_sem.at[p])

    pairs = groups // per
    for p in range(pairs):
        enter(p).start()
    load(0).start()
    for p in range(pairs):
        watch(p).start()
    for c in range(1, min(2, loads)):
        load(c).start()

    barrier = pltpu.get_barrier_semaphore()

    def greet(where):
        pl.semaphore_signal(barrier, inc=1, device_id=where, device_id_type=pl.DeviceIdType.MESH)

    for d in range(1, n_cells):
        greet({"cells": lax.rem(me + d, n_cells)})
    for peer in dp.peer:
        greet({"dp": peer})

    has_under, has_over = me > 0, me < n_cells - 1

    upward = side == 0
    gives = (upward & has_over) | (jnp.logical_not(upward) & has_under)
    takes = (upward & has_under) | (jnp.logical_not(upward) & has_over)

    @pl.when(jnp.logical_not(takes))
    def _():
        rim[...] = jnp.zeros_like(rim)

    for p in range(pairs):
        enter(p).wait()
        turned = flat[:, p * LANES:(p + 1) * LANES].T
        for i in range(per):
            state[0, p * per + i] = turned[i * width:(i + 1) * width]

    pl.semaphore_wait(barrier, n_cells - 1 + len(dp_digits))

    def halo(step, g, i):
        source = (1 - side) * (ncell - plane) + inner
        cols = pl.ds(pl.multiple_of(i * (width // PIECES), 8), width // PIECES)
        return pltpu.make_async_remote_copy(
            src_ref=state.at[step, g, cols, lanes(source, seg)],
            dst_ref=rim.at[step, g, cols],
            send_sem=h_send.at[step, g * PIECES + i],
            recv_sem=h_recv.at[step, g * PIECES + i],
            device_id={"cells": me + 1 - 2 * side},
            device_id_type=pl.DeviceIdType.MESH,
        )

    def border(step, g, i):
        @pl.when(gives)
        def _():
            halo(step, g, i).start()

    def predict(step, g, c):
        p, i = over(g, per)
        at = pl.ds(pl.multiple_of(c * rows, LANES), rows)
        joint = (step == 0) & (i == 0)
        top = pl.ds(pl.multiple_of(i * width, 16), width)
        low = pl.ds(pl.multiple_of(LANES + i * width, 16), width)

        @pl.when((c == 0) & joint)
        def _():
            for n in range(per):
                hi, lo = split(state[0, g + n])
                wide[p, n * width:(n + 1) * width, :] = hi
                wide[p, LANES + n * width:LANES + (n + 1) * width, :] = lo

        @pl.when((c == 0) & (step > 0))
        def _():
            hi, lo = split(state[step, g])
            wide[p, top, :] = hi
            wide[p, low, :] = lo

        @pl.when((step == 0) & (g == 0))
        def _():
            for n in range(rows // batch):
                b = c * (rows // batch) + n
                load(b).wait()
                into = pl.ds(pl.multiple_of(b * batch, LANES), batch)
                hi, lo = split(sens[lax.rem(b, 2)])
                s_high[into, :] = hi
                s_low[into, :] = lo

                @pl.when(b + 2 < loads)
                def _():
                    load(b + 2).start()

        @pl.when(joint)
        def _():
            both = dot(wide[p], s_high[at, :], nt)
            total = both[:LANES] + both[LANES:] + dot(wide[p, :LANES, :], s_low[at, :], nt)
            for n in range(per):
                part[g + n, :, at] = total[n * width:(n + 1) * width]

        @pl.when(step > 0)
        def _():
            hi = wide[p, top, :]
            both = dot(jnp.concatenate([hi, wide[p, low, :]], axis=0), t_high[:, at], nn)
            part[g, :, at] = both[:width] + both[width:] + dot(hi, t_low[:, at], nn)

    def turn(step, g, c):
        @pl.when((step == 0) & (g == 1))
        def _():
            at = pl.ds(pl.multiple_of(c * rows, LANES), rows)
            t_high[:, at] = s_high[at, :].T
            t_low[:, at] = s_low[at, :].T

    def sight(step, g, c):
        @pl.when((step == 0) & (g < pairs))
        def _():
            p = g

            @pl.when(c == 0)
            def _():
                watch(p).wait()

            at = lanes(c * rows, rows)
            turned = obs_raw[at, lanes(p * LANES, LANES)].T
            for i in range(per):
                obs[p * per + i, :, at] = turned[i * width:(i + 1) * width]

    def back(step, g, c):
        @pl.when(c == 0)
        def _():
            grad[g] = jnp.zeros_like(grad[g])

        at = pl.ds(pl.multiple_of(c * rows, LANES), rows)
        hi, lo = split(weighted[g, :, at])
        both = dot(jnp.concatenate([hi, lo], axis=0), s_high[at, :], nn)
        grad[g] += both[:width] + both[width:] + dot(hi, s_low[at, :], nn)

    def smooth_part(step, g, k):
        p, i = over(g, per)

        @pl.when(i == per - 1)
        def _():
            smooth_pair(step, p, k)

    def smooth_pair(step, p, k):
        @pl.when((step == 0) & (p == 0))
        def _():
            row = near_ref[pl.ds(k, 1), lanes(inner, seg)]
            chosen = lax.broadcasted_iota(jnp.int32, (plane, seg), 0) == row
            pick[k] = jnp.where(chosen, 1.0, 0.0).astype(BF16)

        mine = pl.ds(p * per, per)
        cell = state[step, mine, :, lanes(own, seg)]

        def pull(other):
            diff = other - cell
            return diff / jnp.sqrt(1.0 + diff * diff)

        @pl.when(k == 0)
        def _():
            @pl.when(gives)
            def _():
                for n in range(per):
                    for i in range(PIECES):
                        halo(step, p * per + n, i).wait_send()

            @pl.when(takes)
            def _():
                for n in range(per):
                    for i in range(PIECES):
                        halo(step, p * per + n, i).wait_recv()

            beside = state[step, mine, :, lanes((1 - side) * prow + inner, seg)]
            smooth[mine] = pull(rim[step, mine]) + pull(beside)

        both = dot(wide[p, :, lanes(side * plane, plane)], pick[k], nn)
        other = (both[:LANES] + both[LANES:]).reshape(per, width, seg)
        scale = jnp.where(k == 3, 0.05 * (1.0 - 0.75 * mask_ref[:, lanes(own, seg)].astype(F32)), 1.0)
        smooth[mine] = (smooth[mine] + pull(other)) * scale

    def at_slot(x, count, stride, act):
        step = sum((x >= i * period).astype(jnp.int32) for i in range(1, ITERS))
        g, place = over(x - step * period, span)
        index, wait = over(place, stride)

        @pl.when((x >= 0) & (g < groups) & (index < count) & (wait == 0))
        def _():
            act(step, g, index)

    def cell_stage(s, step, g, c):
        def reweight(cols, at, total):
            misfit = total - obs[g, cols, at]
            weighted[g, cols, at] = misfit / jnp.maximum(jnp.abs(misfit), 1.0)

        for way in ways:
            way.stage(s, c, step * units + g * chunks + c, part.at[g], land.at[step, g], weighted.at[g], reweight)

    def dp_stage(s, step, g, q):
        def blend():
            @pl.when(side == q)
            def _():
                grad[g, :, lanes(own, seg)] -= smooth[g]

        def update(cols, at, total):
            state[step + 1, g, :, at] = state[step, g, :, at] - 1.0 * total

        slot = (step * groups + g) * parts + q
        dp.stage(s, q, slot, grad.at[g], gland.at[step, g], state.at[step + 1, g], update, blend)

    def depart(step, g, i):
        @pl.when((step == ITERS - 1) & (lax.rem(g, per) == per - 1))
        def _():
            p = lax.div(g, per)
            rest = [state[ITERS, g - per + 1 + i] for i in range(per)]
            flat[:, lanes(p * LANES, LANES)] = jnp.concatenate(rest, axis=0).T
            leave(p).start()

    def slot(t, carry):
        for s in reversed(range(cells.stages + 1)):
            at_slot(t - cell_at[s], chunks, STRIDE, functools.partial(cell_stage, s))
        for s in reversed(range(dp.stages + 1)):
            at_slot(t - delay - dp_at[s], parts, 1, functools.partial(dp_stage, s))
        at_slot(t + 1, chunks, STRIDE, predict)
        at_slot(t - HALO_LAG, PIECES, HALO_STRIDE, border)
        at_slot(t, chunks, STRIDE, sight)
        at_slot(t + 1 - TURN_LAG, chunks, STRIDE, turn)
        at_slot(t - SMOOTH_LAG, 4, 1, smooth_part)
        at_slot(t - behind, chunks, STRIDE, back)
        at_slot(t - done + 1, 1, 1, depart)
        return carry

    lax.fori_loop(-1, slots, slot, 0)
    for p in range(pairs):
        leave(p).wait()


def invert(n_dp, n_cells, sensitivity, observed, models, neighbour_map, edge_mask):
    ndata, ncell = sensitivity.shape
    total = models.shape[1]
    width = total // GROUPS
    plane = neighbour_map.shape[1]
    nb, nd = 2 * len(digits_of(n_cells)) - 1, 2 * len(digits_of(n_dp)) - 1
    chunks = ndata // max(CHUNK, LANES * n_cells // 2)
    parts = ncell // plane
    seg = ncell // n_dp
    copies = 11 if n_cells == 8 else nb
    vmem = pl.BlockSpec(memory_space=pltpu.VMEM)
    hbm = pl.BlockSpec(memory_space=pl.ANY)
    dma = pltpu.SemaphoreType.DMA
    return pl.pallas_call(
        functools.partial(body, (n_dp, n_cells), plane),
        out_shape=jax.ShapeDtypeStruct(models.shape, F32),
        in_specs=[hbm] * 3 + [vmem] * 2,
        out_specs=hbm,
        scratch_shapes=[
            pltpu.VMEM((2, LOAD, ncell), F32),
            pltpu.VMEM((ndata, ncell), BF16),
            pltpu.VMEM((ndata, ncell), BF16),
            pltpu.VMEM((ncell, ndata), BF16),
            pltpu.VMEM((ncell, ndata), BF16),
            pltpu.VMEM((ndata, total), F32),
            pltpu.VMEM((GROUPS, width, ndata), F32),
            pltpu.VMEM((GROUPS, width, ndata), F32),
            pltpu.VMEM((ITERS, GROUPS, width, 2 * ndata), F32),
            pltpu.VMEM((GROUPS, width, ndata), F32),
            pltpu.VMEM((GROUPS, width, ncell), F32),
            pltpu.VMEM((ITERS, GROUPS, width, ncell), F32),
            pltpu.VMEM((ncell, total), F32),
            pltpu.VMEM((ITERS + 1, GROUPS, width, ncell), F32),
            pltpu.VMEM((GROUPS * width // LANES, 2 * LANES, ncell), BF16),
            pltpu.VMEM((4, plane, seg), BF16),
            pltpu.VMEM((GROUPS, width, seg), F32),
            pltpu.VMEM((ITERS, GROUPS, width, seg), F32),
            dma((ndata // LOAD,)),
            dma((GROUPS * width // LANES,)),
            dma((GROUPS * width // LANES,)),
            dma((copies, ITERS * GROUPS * chunks)),
            dma((copies, ITERS * GROUPS * chunks)),
            dma((nd, ITERS * GROUPS * parts)),
            dma((nd, ITERS * GROUPS * parts)),
            dma((ITERS, GROUPS * PIECES)),
            dma((ITERS, GROUPS * PIECES)),
        ],
        compiler_params=pltpu.CompilerParams(
            collective_id=0, has_side_effects=True, vmem_limit_bytes=67043328
        ),
        name="invert",
    )(sensitivity, observed, models, neighbour_map, edge_mask[None, :])


def solution(mesh):
    return jax.shard_map(
        functools.partial(invert, mesh.shape["dp"], mesh.shape["cells"]),
        mesh=mesh,
        in_specs=(P("dp", "cells"), P("dp", None), P("cells", None), P(), P("cells")),
        out_specs=P("cells", None),
        check_vma=False,
    )
```
